32 devices in a mesh: page: 8 (over y, x, core), blk: 4 (over z).
Axes of the slice: x: 2, y: 2, z: 4, core: 2. Of those that a mesh axis runs over, the one named last changes fastest.
Arguments:
- tokens: bfloat16 [8, 2048, 1024], P('page', 'blk'), may hold values from -6 to 6
- patches: bfloat16 [8, 1024, 1024], P('page', 'blk'), may hold values from -6 to 6
- patch_mask: int32 [8, 1024], P('page', 'blk'), may hold values from 0 to 1, as said below
- gain_one: float32 [1024], replicated, may hold values from 0.1 to 1.9
- qkv_self: bfloat16 [1024, 3072], replicated, may hold values from -0.1875 to 0.1875
- out_self: bfloat16 [1024, 1024], replicated, may hold values from -1.5 to 1.5
- gain_two: float32 [1024], replicated, may hold values from 0.1 to 1.9
- q_cross: bfloat16 [1024, 1024], replicated, may hold values from -0.1875 to 0.1875
- kv_cross: bfloat16 [1024, 2048], replicated, may hold values from -0.1875 to 0.1875
- out_cross: bfloat16 [1024, 1024], replicated, may hold values from -1.5 to 1.5
- gain_three: float32 [1024], replicated, may hold values from 0.1 to 1.9
- w_up: bfloat16 [1024, 4096], replicated, may hold values from -0.1875 to 0.1875
- w_down: bfloat16 [4096, 1024], replicated, may hold values from -0.09375 to 0.09375
- cotangent: bfloat16 [8, 2048, 1024], P('page', 'blk'), may hold values from -6 to 6
Outputs:
- output: bfloat16 [8, 2048, 1024], P('page', 'blk')
- grad_tokens: float32 [8, 2048, 1024], P('page', 'blk')
- grad_patches: float32 [8, 1024, 1024], P('page', 'blk')
- grad_gain_one: float32 [1024], replicated
- grad_qkv_self: float32 [1024, 3072], P('page', 'blk')
- grad_out_self: float32 [1024, 1024], P('page', 'blk')
- grad_gain_two: float32 [1024], replicated
- grad_q_cross: float32 [1024, 1024], P('page', 'blk')
- grad_kv_cross: float32 [1024, 2048], P('page', 'blk')
- grad_out_cross: float32 [1024, 1024], P('page', 'blk')
- grad_gain_three: float32 [1024], replicated
- grad_w_up: float32 [1024, 4096], P('page', 'blk')
- grad_w_down: float32 [4096, 1024], P('page', 'blk')
The draws below stay inside these ranges and needn't reach their ends.
Inputs may be any that keep to these rules, and one draw needn't show every extreme that they name: `patch_mask`: 1 keeps a patch and 0 excludes it; the excluded patches of a page form one rectangle of its grid of 16 rows and 64 columns, of at most half of the rows and at most 32 columns.
All inputs are finite; a program needn't handle non-finite values.
Results may differ from the reference program's by a relative error of at most 0.025.
Values may be sent and summed in bfloat16 or wider, within the bound.
No kernel may reach another device: no remote copies, remote signals or barrier semaphores. Data moves between devices by JAX's collectives and lax.ppermute only.
A program may use at most 384 MiB of HBM per device.

```python
import jax
import jax.numpy as jnp
from jax import lax

D = 1024
HEADS = 16
HEAD_DIM = 64
FF = 4096
SEQ = 2048
PATCHES = 1024
PAGES = 8


def draw_patch_mask(key, part):
    grid_rows = PATCHES // 64
    subkeys = jax.random.split(key, 4)
    row_start = jax.random.randint(subkeys[0], (PAGES, 1, 1), 0, grid_rows)
    row_count = jax.random.randint(subkeys[1], (PAGES, 1, 1), 1, grid_rows // 2 + 1)
    col_start = jax.random.randint(subkeys[2], (PAGES, 1, 1), 0, 64)
    col_count = jax.random.randint(subkeys[3], (PAGES, 1, 1), 8, 33)
    row_place = jnp.arange(grid_rows, dtype=jnp.int32).reshape(1, grid_rows, 1)
    column_place = jnp.arange(64, dtype=jnp.int32).reshape(1, 1, 64)
    in_rows = (row_place >= row_start) & (row_place < row_start + row_count)
    in_columns = (column_place >= col_start) & (column_place < col_start + col_count)
    blank = in_rows & in_columns
    return jnp.where(blank, 0, 1).astype(jnp.int32).reshape(PAGES, PATCHES)


def level_of(rng, dims, cuts, smallest, high):
    def one(position, shards_of):
        draws = jax.random.uniform(jax.random.fold_in(jax.random.fold_in(rng, 6), position), (shards_of,), jnp.float32, smallest / len(cuts), high / len(cuts))
        return jnp.repeat(jnp.exp(draws), dims[position] // shards_of).reshape((-1,) + (1,) * (len(dims) - position - 1))

    loudness = one(*cuts[0])
    for cut in cuts[1:]:
        loudness = loudness * one(*cut)
    return loudness


def bell_draw(rng, shape, width, bound, cuts=(), kind=jnp.bfloat16):
    loudness = level_of(rng, shape, cuts, -0.22, 0.18) if cuts else 1.0
    values = jax.random.normal(rng, shape, jnp.float32) * width * loudness
    return jnp.minimum(jnp.maximum(values, -bound), bound).astype(kind)


def setup_inputs(seed: int = 0) -> dict:
    key_list = jax.random.split(jax.random.key(seed), 15)
    tokens = bell_draw(key_list[0], (PAGES, SEQ, D), 1.0, 6.0, ((0, 8), (1, 4)))
    patches = bell_draw(key_list[1], (PAGES, PATCHES, D), 1.0, 6.0, ((0, 8), (1, 4)))
    patch_mask = draw_patch_mask(jax.random.fold_in(key_list[14], 71), 0)
    gain_one = jnp.clip(1.0 + 0.18 * jax.random.normal(key_list[3], (D,), jnp.float32), 0.1, 1.9)
    qkv_self = bell_draw(key_list[4], (D, 3 * D), D ** -0.5, 0.1875)
    out_self = bell_draw(key_list[5], (D, D), (D // 64) ** -0.5, 1.5)
    gain_two = jnp.clip(1.0 + 0.18 * jax.random.normal(key_list[6], (D,), jnp.float32), 0.1, 1.9)
    q_cross = bell_draw(key_list[7], (D, D), D ** -0.5, 0.1875)
    kv_cross = bell_draw(key_list[8], (D, 2 * D), D ** -0.5, 0.1875)
    out_cross = bell_draw(key_list[9], (D, D), (D // 64) ** -0.5, 1.5)
    gain_three = jnp.clip(1.0 + 0.18 * jax.random.normal(key_list[10], (D,), jnp.float32), 0.1, 1.9)
    w_up = bell_draw(key_list[11], (D, FF), D ** -0.5, 0.1875)
    w_down = bell_draw(key_list[12], (FF, D), FF ** -0.5, 0.09375)
    cotangent = bell_draw(key_list[13], (PAGES, SEQ, D), 1.0, 6.0, ((0, 8), (1, 4)))
    return dict(tokens=tokens, patches=patches, patch_mask=patch_mask, gain_one=gain_one, qkv_self=qkv_self, out_self=out_self, gain_two=gain_two, q_cross=q_cross, kv_cross=kv_cross, out_cross=out_cross, gain_three=gain_three, w_up=w_up, w_down=w_down, cotangent=cotangent)


@jax.custom_vjp
def low(v):
    return lax.optimization_barrier(v.astype(jnp.bfloat16)).astype(jnp.float32)

@jax.custom_vjp
def low_back(v):
    return v

def low_keep(v):
    return (low(v), None)

def low_pass(kept, grad):
    return (grad,)

def back_keep(v):
    return (v, None)

def back_low(kept, grad):
    return (low(grad),)
low.defvjp(low_keep, low_pass)
low_back.defvjp(back_keep, back_low)
norm_eps = 1e-05
masked_score = -1e+30
highest = lax.Precision.HIGHEST

def matmul(left, right):
    return jnp.dot(left, right, precision=highest)

def both_ways(values):
    return low_back(low(values))

def layer_norm(values, gain_row):
    center = values - lax.optimization_barrier(jnp.mean(values, axis=-1, keepdims=True))
    variance = lax.optimization_barrier(jnp.mean(center * center, axis=-1, keepdims=True))
    return center * lax.rsqrt(variance + norm_eps) * gain_row

def attention(queries, key_rows, value_rows, allowed):
    row_count = queries.shape[0]
    query_heads = queries.reshape(row_count, HEADS, HEAD_DIM).transpose(1, 0, 2)
    key_heads = key_rows.reshape(-1, HEADS, HEAD_DIM).transpose(1, 0, 2)
    value_heads = value_rows.reshape(-1, HEADS, HEAD_DIM).transpose(1, 0, 2)

    def one_head(triple):
        head_query, head_key, head_value = triple
        scores = low_back(jnp.dot(head_query, head_key.T, precision=highest) * HEAD_DIM ** (-0.5))
        scores = jnp.where(allowed, scores, masked_score)
        shares = low(jax.nn.softmax(scores, axis=-1))
        return jnp.dot(shares, head_value, precision=highest)
    blended = lax.map(jax.checkpoint(one_head), (query_heads, key_heads, value_heads))
    return blended.transpose(1, 0, 2).reshape(row_count, -1)

def layer_forward(params, token_rows, patch_rows, live_mask):
    gain_one, qkv_self, out_self, gain_two, q_cross, kv_cross, out_cross, gain_three, w_up, w_down = params
    positions = jnp.arange(token_rows.shape[0])
    causal = positions[:, None] >= positions[None, :]
    normed_one = low(layer_norm(token_rows, gain_one))
    packed = both_ways(matmul(normed_one, qkv_self))
    mixed_one = both_ways(attention(packed[:, :D], packed[:, D:2 * D], packed[:, 2 * D:], causal))
    resid_one = token_rows + low_back(matmul(mixed_one, out_self))
    normed_two = low(layer_norm(resid_one, gain_two))
    query_two = both_ways(matmul(normed_two, q_cross))
    pair_two = both_ways(matmul(patch_rows, kv_cross))
    mixed_two = both_ways(attention(query_two, pair_two[:, :D], pair_two[:, D:], live_mask[None, :] > 0))
    resid_two = resid_one + low_back(matmul(mixed_two, out_cross))
    normed_three = low(layer_norm(resid_two, gain_three))
    upward = low_back(matmul(normed_three, w_up))
    active = low(jax.nn.gelu(upward, approximate=False))
    return resid_two + low_back(matmul(active, w_down))

def reference(tokens, patches, patch_mask, gain_one, qkv_self, out_self, gain_two, q_cross, kv_cross, out_cross, gain_three, w_up, w_down, cotangent):
    params = tuple((tensor.astype(jnp.float32) for tensor in (gain_one, qkv_self, out_self, gain_two, q_cross, kv_cross, out_cross, gain_three, w_up, w_down)))

    def page_step(totals, page_data):
        page_tokens, page_patches, page_live, page_cot = page_data

        def forward(weights, token_rows, patch_rows):
            return layer_forward(weights, token_rows, patch_rows, page_live)
        result, pullback = jax.vjp(forward, params, page_tokens.astype(jnp.float32), page_patches.astype(jnp.float32))
        d_params, d_tokens, d_patches = pullback(page_cot.astype(jnp.float32))
        totals = jax.tree.map(jnp.add, totals, d_params)
        return (totals, (result.astype(jnp.bfloat16), d_tokens, d_patches))
    start = jax.tree.map(jnp.zeros_like, params)
    totals, (output, grad_tokens, grad_patches) = lax.scan(page_step, start, (tokens, patches, patch_mask, cotangent))
    grad_gain_one, grad_qkv_self, grad_out_self, grad_gain_two, grad_q_cross, grad_kv_cross, grad_out_cross, grad_gain_three, grad_w_up, grad_w_down = totals
    return (output, grad_tokens, grad_patches, grad_gain_one, grad_qkv_self, grad_out_self, grad_gain_two, grad_q_cross, grad_kv_cross, grad_out_cross, grad_gain_three, grad_w_up, grad_w_down)
```

```python
import functools

import jax
import jax.numpy as jnp
from jax import lax
from jax.experimental import pallas as pl
from jax.experimental.pallas import tpu as pltpu
from jax.sharding import PartitionSpec as P

HEADS = 16
HEAD_DIM = 64
LANES = 128

norm_eps = 1e-05
masked_score = -1e30


def nt(left, right):
    return lax.dot_general(
        left, right, (((1,), (1,)), ((), ())), preferred_element_type=jnp.float32
    )


def nn(left, right):
    return lax.dot_general(
        left, right, (((1,), (0,)), ((), ())), preferred_element_type=jnp.float32
    )


def tn(left, right):
    return lax.dot_general(
        left, right, (((0,), (0,)), ((), ())), preferred_element_type=jnp.float32
    )


def lane_of(shape):
    return lax.broadcasted_iota(jnp.int32, shape, len(shape) - 1)


def own_lanes(shape, head):
    lane = lane_of(shape)
    return lane < HEAD_DIM if head == 0 else lane >= HEAD_DIM


def spare_lane(shape, head):
    return lane_of(shape) - (HEAD_DIM if head == 0 else 0)


def three_parts(column):
    high = column.astype(jnp.bfloat16)
    rest = column - high.astype(jnp.float32)
    middle = rest.astype(jnp.bfloat16)
    low = (rest - middle.astype(jnp.float32)).astype(jnp.bfloat16)
    return high, middle, low


def forward_kernel(heads, causal, tq, tk, q_ref, k_ref, v_ref, *rest):
    if causal:
        bias_ref = None
        mixed_ref, qx_ref, kx, vx = rest
    else:
        bias_ref, mixed_ref, qx_ref, kx, vx = rest
    step = pl.program_id(2)
    keys = k_ref.shape[0]
    scale = HEAD_DIM ** (-0.5)

    @pl.when(step == 0)
    def _():
        turned = v_ref[...].astype(jnp.float32).T.astype(jnp.bfloat16)
        ones = jnp.ones((16, keys), jnp.bfloat16)
        for h in range(heads):
            vx[h, :HEAD_DIM] = turned[h * HEAD_DIM : (h + 1) * HEAD_DIM]
            vx[h, HEAD_DIM:] = ones
            k = k_ref[...]
            filler = jnp.zeros_like(k) if causal else bias_ref[...]
            kx[h] = jnp.where(own_lanes(k.shape, h), k, filler)

    q = q_ref[...] * jnp.bfloat16(scale)
    q_heads = []
    for h in range(heads):
        one = (spare_lane(q.shape, h) == 0).astype(jnp.float32).astype(jnp.bfloat16)
        q_heads.append(jnp.where(own_lanes(q.shape, h), q, one))

    def tile(j, carry, masked):
        out = []
        start = pl.multiple_of(j * tk, tk)
        for h in range(heads):
            largest, total = carry[h]
            scores = nt(kx[h, pl.ds(start, tk), :], q_heads[h])
            if masked:
                key_at = start + lax.broadcasted_iota(jnp.int32, scores.shape, 0)
                query_at = step * tq + lax.broadcasted_iota(jnp.int32, scores.shape, 1)
                scores = jnp.where(key_at <= query_at, scores, masked_score)
            new_largest = jnp.maximum(largest, jnp.max(scores, axis=0, keepdims=True))
            raised = jnp.exp(scores - new_largest).astype(jnp.bfloat16)
            part = nn(vx[h, :, pl.ds(start, tk)], raised)
            out.append((new_largest, total * jnp.exp(largest - new_largest) + part))
        return tuple(out)

    carry = tuple(
        (
            jnp.full((1, tq), masked_score, jnp.float32),
            jnp.zeros((HEAD_DIM + 16, tq), jnp.float32),
        )
        for _ in range(heads)
    )
    if causal:
        full = step * tq // tk
        carry = lax.fori_loop(0, full, lambda j, c: tile(j, c, False), carry)
        for extra in range(max(tq // tk, 1)):
            carry = tile(full + extra, carry, True)
    else:
        for j in range(keys // tk):
            carry = tile(j, carry, False)
    blended, columns = [], []
    for h in range(heads):
        largest, total = carry[h]
        sums = total[HEAD_DIM : HEAD_DIM + 1]
        blended.append(total[:HEAD_DIM] / sums)
        columns.append(-(largest + jnp.log(sums)))
    if heads == 1:
        blended.append(jnp.zeros_like(blended[0]))
    mixed_ref[...] = jnp.concatenate(blended, 0).T.astype(mixed_ref.dtype)
    for h in range(heads):
        turned = jnp.broadcast_to(columns[h], (LANES, tq)).T
        high, middle, low = three_parts(turned)
        place = spare_lane(q.shape, h)
        qx = jnp.where(own_lanes(q.shape, h), q, jnp.zeros_like(q))
        qx = jnp.where(place == 0, jnp.ones_like(q), qx)
        qx = jnp.where(place == 1, high, qx)
        qx = jnp.where(place == 2, middle, qx)
        qx_ref[:, h * LANES : (h + 1) * LANES] = jnp.where(place == 3, low, qx)


def backward_kernel(heads, causal, tq, tk, qx_ref, k_ref, v_ref, o_ref, do_ref, *rest):
    bias_ref = None
    if causal:
        packed_ref, kx, kt, vx, dx, dqt = rest
    else:
        bias_ref, dq_ref, packed_ref, kx, kt, vx, dx, dqt = rest
    queries, keys = qx_ref.shape[0], k_ref.shape[0]
    scale = HEAD_DIM ** (-0.5)
    at = LANES if causal else 0

    k = k_ref[...]
    v = v_ref[...]
    kt[...] = (k.astype(jnp.float32) * scale).T.astype(jnp.bfloat16)
    do = do_ref[...]
    product = do.astype(jnp.float32) * o_ref[...].astype(jnp.float32)
    for h in range(heads):
        own = own_lanes(k.shape, h)
        place = spare_lane(k.shape, h)
        ones = jnp.ones_like(k)
        bias = jnp.zeros_like(k) if causal else bias_ref[...]
        kx[h] = jnp.where(own, k, jnp.where(place == 0, bias, ones))
        vx[h] = jnp.where(own, v, ones)
        own = own_lanes(do.shape, h)
        place = spare_lane(do.shape, h)
        delta = jnp.sum(jnp.where(own, product, 0.0), axis=1, keepdims=True)
        high, middle, low = three_parts(jnp.broadcast_to(-delta, do.shape))
        value = jnp.where(own, do, jnp.zeros_like(do))
        value = jnp.where(place == 0, high, value)
        value = jnp.where(place == 1, middle, value)
        dx[h] = jnp.where(place == 2, low, value)

    dqt[...] = jnp.zeros_like(dqt)

    def tile(i, j, masked, sums):
        q_at = pl.multiple_of(i * tq, tq)
        k_at = pl.multiple_of(j * tk, tk)
        out = []
        for h in range(heads):
            qx = qx_ref[pl.ds(q_at, tq), h * LANES : (h + 1) * LANES]
            shares = jnp.exp(nt(kx[h, pl.ds(k_at, tk), :], qx))
            if masked:
                key_at = k_at + lax.broadcasted_iota(jnp.int32, shares.shape, 0)
                query_at = q_at + lax.broadcasted_iota(jnp.int32, shares.shape, 1)
                shares = jnp.where(key_at <= query_at, shares, 0.0)
            grad = dx[h, pl.ds(q_at, tq), :]
            d_shares = nt(vx[h, pl.ds(k_at, tk), :], grad)
            d_scores = (shares * d_shares).astype(jnp.bfloat16)
            dv = nn(shares.astype(jnp.bfloat16), grad)
            dk = nn(d_scores, qx)
            rows = pl.ds(h * HEAD_DIM, HEAD_DIM)
            dqt[rows, pl.ds(q_at, tq)] += nn(kt[rows, pl.ds(k_at, tk)], d_scores)
            if sums is not None:
                dk, dv = sums[h][0] + dk, sums[h][1] + dv
            out.append((dk, dv))
        return tuple(out)

    def finish(j, sums):
        k_at = pl.multiple_of(j * tk, tk)
        dk, dv = sums[0]
        if heads == 2:
            own = own_lanes(dk.shape, 0)
            dk, dv = jnp.where(own, dk, sums[1][0]), jnp.where(own, dv, sums[1][1])
        packed_ref[pl.ds(k_at, tk), at : at + LANES] = dk.astype(packed_ref.dtype)
        packed_ref[pl.ds(k_at, tk), at + LANES : at + 2 * LANES] = dv.astype(packed_ref.dtype)

    if causal:

        @pl.loop(0, keys // tk)
        def _(j):
            sums = tile(j, j, True, None)
            sums = lax.fori_loop(
                j + 1, queries // tq, lambda i, s: tile(i, j, False, s), sums
            )
            finish(j, sums)

        packed_ref[:, :LANES] = dqt[...].T.astype(packed_ref.dtype)
    else:
        for j in range(keys // tk):
            sums = None
            for i in range(queries // tq):
                sums = tile(i, j, False, sums)
            finish(j, sums)
        dq_ref[...] = dqt[...].T.astype(dq_ref.dtype)


def tile_of(rows, largest):
    return rows if rows < largest else largest


def attend(q, kv, bias, heads, blocks, tq, tk):
    pages, queries = q.shape[:2]
    keys = kv.shape[1]
    causal = bias is None
    tq, tk = tile_of(queries, tq), tile_of(keys, tk)
    wide, skip = (3, 1) if causal else (2, 0)
    q_wide = 3 if causal else 1
    in_specs = [
        pl.BlockSpec((None, tq, LANES), lambda p, b, i: (p, i, q_wide * b)),
        pl.BlockSpec((None, keys, LANES), lambda p, b, i: (p, 0, wide * b + skip)),
        pl.BlockSpec((None, keys, LANES), lambda p, b, i: (p, 0, wide * b + skip + 1)),
    ]
    args = [q, kv, kv]
    if not causal:
        in_specs.append(pl.BlockSpec((None, keys, LANES), lambda p, b, i: (p, 0, 0)))
        args.append(bias)
    elements = pages * blocks * heads * queries * keys // (2 if causal else 1)
    return pl.pallas_call(
        functools.partial(forward_kernel, heads, causal, tq, tk),
        grid=(pages, blocks, queries // tq),
        in_specs=in_specs,
        out_specs=[
            pl.BlockSpec((None, tq, LANES), lambda p, b, i: (p, i, b)),
            pl.BlockSpec((None, tq, heads * LANES), lambda p, b, i: (p, i, b)),
        ],
        out_shape=[
            jax.ShapeDtypeStruct((pages, queries, blocks * LANES), jnp.bfloat16),
            jax.ShapeDtypeStruct((pages, queries, blocks * heads * LANES), jnp.bfloat16),
        ],
        scratch_shapes=[
            pltpu.VMEM((heads, keys, LANES), jnp.bfloat16),
            pltpu.VMEM((heads, HEAD_DIM + 16, keys), jnp.bfloat16),
        ],
        compiler_params=pltpu.CompilerParams(vmem_limit_bytes=40 << 20),
        cost_estimate=pl.CostEstimate(
            flops=elements * 2048, bytes_accessed=4 << 20, transcendentals=elements
        ),
        name="attend",
    )(*args)


def attend_back(qx, kv, mixed, d_mixed, bias, heads, blocks, tq, tk):
    pages, queries = qx.shape[:2]
    keys = kv.shape[1]
    causal = bias is None
    tq, tk = tile_of(queries, tq), tile_of(keys, tk)
    wide, skip = (3, 1) if causal else (2, 0)
    whole = lambda rows, lanes: pl.BlockSpec((None, rows, lanes), lambda p, b: (p, 0, b))
    in_specs = [
        whole(queries, heads * LANES),
        pl.BlockSpec((None, keys, LANES), lambda p, b: (p, 0, wide * b + skip)),
        pl.BlockSpec((None, keys, LANES), lambda p, b: (p, 0, wide * b + skip + 1)),
        whole(queries, LANES),
        whole(queries, LANES),
    ]
    args = [qx, kv, kv, mixed, d_mixed]
    out_specs = [whole(keys, wide * LANES)]
    out_shape = [jax.ShapeDtypeStruct((pages, keys, blocks * wide * LANES), jnp.bfloat16)]
    if not causal:
        in_specs.append(pl.BlockSpec((None, keys, LANES), lambda p, b: (p, 0, 0)))
        args.append(bias)
        out_specs.insert(0, whole(queries, LANES))
        out_shape.insert(0, jax.ShapeDtypeStruct((pages, queries, blocks * LANES), jnp.bfloat16))
    elements = pages * blocks * heads * queries * keys // (2 if causal else 1)
    return pl.pallas_call(
        functools.partial(backward_kernel, heads, causal, tq, tk),
        grid=(pages, blocks),
        in_specs=in_specs,
        out_specs=out_specs,
        out_shape=out_shape,
        scratch_shapes=[
            pltpu.VMEM((heads, keys, LANES), jnp.bfloat16),
            pltpu.VMEM((LANES, keys), jnp.bfloat16),
            pltpu.VMEM((heads, keys, LANES), jnp.bfloat16),
            pltpu.VMEM((heads, queries, LANES), jnp.bfloat16),
            pltpu.VMEM((LANES, queries), jnp.float32),
        ],
        compiler_params=pltpu.CompilerParams(vmem_limit_bytes=40 << 20),
        cost_estimate=pl.CostEstimate(
            flops=elements * 2560, bytes_accessed=8 << 20, transcendentals=elements
        ),
        name="attend_back",
    )(*args)


def expand_kernel(normed_ref, grad_ref, up_ref, down_ref, active_ref, d_upward_ref):
    upward = nn(normed_ref[...], up_ref[...])
    d_active = nt(grad_ref[...], down_ref[...])
    share = 0.5 * (1.0 + lax.erf(upward * (0.5**0.5)))
    active_ref[...] = (upward * share).astype(active_ref.dtype)
    density = jnp.exp(-0.5 * upward * upward) * 0.3989422804014327
    d_upward_ref[...] = (d_active * (share + upward * density)).astype(d_upward_ref.dtype)


def expand(normed, grad, w_up, w_down):
    rows, width = normed.shape
    wide = w_up.shape[1]
    step = 512
    return pl.pallas_call(
        expand_kernel,
        grid=(wide // step,),
        in_specs=[
            pl.BlockSpec((rows, width), lambda f: (0, 0)),
            pl.BlockSpec((rows, width), lambda f: (0, 0)),
            pl.BlockSpec((width, step), lambda f: (0, f)),
            pl.BlockSpec((step, width), lambda f: (f, 0)),
        ],
        out_specs=[
            pl.BlockSpec((rows, step), lambda f: (0, f)),
            pl.BlockSpec((rows, step), lambda f: (0, f)),
        ],
        out_shape=[jax.ShapeDtypeStruct((rows, wide), jnp.bfloat16)] * 2,
        compiler_params=pltpu.CompilerParams(vmem_limit_bytes=40 << 20),
        cost_estimate=pl.CostEstimate(
            flops=4 * rows * width * wide, bytes_accessed=26 << 20, transcendentals=2 * rows * wide
        ),
        name="expand",
    )(normed, grad, w_up, w_down)


def norm_of(values):
    center = values - jnp.mean(values, axis=-1, keepdims=True)
    rstd = lax.rsqrt(jnp.mean(center * center, axis=-1, keepdims=True) + norm_eps)
    return center * rstd, rstd


def norm_back(values, gain, d_normed):
    xhat, rstd = norm_of(values)
    e = d_normed * gain
    d_values = rstd * (
        e
        - jnp.mean(e, axis=-1, keepdims=True)
        - xhat * jnp.mean(e * xhat, axis=-1, keepdims=True)
    )
    return d_values, jnp.sum(d_normed * xhat, axis=0)


def shifted(value, shift):
    count = lax.axis_size("blk")
    return lax.ppermute(value, "blk", [(i, (i + shift) % count) for i in range(count)])


def ring_pieces(value):
    count = lax.axis_size("blk")
    pieces = [(value, 0)]
    right = left = value
    for hop in range(1, (count - 1) // 2 + 1):
        right, left = shifted(right, 1), shifted(left, -1)
        pieces += [(right, -hop), (left, hop)]
    if count % 2 == 0:
        half = value.shape[1] // 2
        if count > 1:
            top, low = shifted(right[:, :half], 1), shifted(left[:, half:], -1)
            pieces.append((jnp.concatenate([top, low], 1), count // 2))
    return pieces


def gathered(pieces, axis):
    count = lax.axis_size("blk")
    place = lax.axis_index("blk")
    size = pieces[0][0].shape[axis]
    shape = list(pieces[0][0].shape)
    shape[axis] = size * count
    whole = jnp.zeros(shape, pieces[0][0].dtype)
    for piece, far in pieces:
        whole = lax.dynamic_update_slice_in_dim(
            whole, piece, (place + far) % count * size, axis
        )
    return whole


def exchanged(value, split, join):
    count = lax.axis_size("blk")
    place = lax.axis_index("blk")
    size = value.shape[split] // count
    take = lambda far: lax.dynamic_slice_in_dim(
        value, (place + far) % count * size, size, split
    )
    pieces = [(take(0), 0)]
    order = sorted(range(1, count), key=lambda far: -min(far, count - far))
    for far in order:
        pieces.append((shifted(take(far), far), -far))
    return gathered(pieces, join)


def on_device(
    tokens,
    patches,
    patch_mask,
    gain_one,
    qkv_self,
    out_self,
    gain_two,
    q_cross,
    kv_cross,
    out_cross,
    gain_three,
    w_up,
    w_down,
    cotangent,
):
    pages, token_count, width = tokens.shape
    patch_count = patches.shape[1]
    count = lax.axis_size("blk")
    place = lax.axis_index("blk")
    rows = pages * token_count
    here = HEADS // count
    heads = 2 if here % 2 == 0 else 1
    blocks = here // heads
    lanes = heads * HEAD_DIM

    def padded(value):
        if lanes == LANES:
            return value
        split = value.reshape(value.shape[:-1] + (-1, lanes))
        split = jnp.pad(split, [(0, 0)] * (split.ndim - 1) + [(0, LANES - lanes)])
        return split.reshape(value.shape[:-1] + (-1,))

    def cut(value):
        if lanes == LANES:
            return value
        split = value.reshape(value.shape[:-1] + (-1, LANES))[..., :lanes]
        return split.reshape(value.shape[:-1] + (-1,))

    qkv_blocks = (
        qkv_self.reshape(width, 3, width // lanes, lanes)
        .transpose(0, 2, 1, 3)
        .reshape(width, 3 * width)
    )
    qkv_here = lax.dynamic_slice_in_dim(
        qkv_blocks, place * (3 * width // count), 3 * width // count, 1
    )
    kv_blocks = (
        kv_cross.reshape(width, 2, width // LANES, LANES)
        .transpose(0, 2, 1, 3)
        .reshape(width, 2 * width)
    )

    normed_pieces, packed_pieces = [], []
    for piece, far in ring_pieces(tokens):
        flat = piece.reshape(rows, width).astype(jnp.float32)
        normed = (norm_of(flat)[0] * gain_one).astype(jnp.bfloat16)
        packed = padded(nn(normed, qkv_here).astype(jnp.bfloat16))
        normed_pieces.append((normed.reshape(pages, token_count, width), far))
        packed_pieces.append((packed.reshape(pages, token_count, -1), far))
    normed_one = gathered(normed_pieces, 1)
    packed = gathered(packed_pieces, 1)
    mixed_here, qx_one = attend(packed, packed, None, heads, blocks, 512, 512)
    mixed_one = exchanged(cut(mixed_here), 1, 2).reshape(rows, width)

    patches_all = gathered(ring_pieces(patches), 1)
    dead = jnp.where(patch_mask > 0, 0.0, masked_score).astype(jnp.bfloat16)
    dead_pieces = [(dead, 0)] + [(shifted(dead, far), -far) for far in range(1, count)]
    bias = gathered(dead_pieces, 1)
    bias = jnp.broadcast_to(bias[:, :, None], bias.shape + (LANES,))
    page_patches = patches_all.reshape(-1, width)
    kv_two = nn(page_patches, kv_blocks).astype(jnp.bfloat16)
    kv_two = kv_two.reshape(pages, -1, 2 * width)

    flat_tokens = tokens.reshape(rows, width).astype(jnp.float32)
    resid_one = flat_tokens + nn(mixed_one, out_self)
    normed_two = (norm_of(resid_one)[0] * gain_two).astype(jnp.bfloat16)
    query_two = nn(normed_two, q_cross).astype(jnp.bfloat16).reshape(pages, token_count, width)
    mixed_two, qx_two = attend(query_two, kv_two, bias, 2, width // LANES, 512, 1024)
    flat_mixed_two = mixed_two.reshape(rows, width)
    resid_two = resid_one + nn(flat_mixed_two, out_cross)
    normed_three = (norm_of(resid_two)[0] * gain_three).astype(jnp.bfloat16)

    flat_cotangent = cotangent.reshape(rows, width)
    active, d_upward = expand(normed_three, flat_cotangent, w_up, w_down)
    output = (resid_two + nn(active, w_down)).astype(jnp.bfloat16)
    grad_w_down = tn(active, flat_cotangent)
    grad_w_up = tn(normed_three, d_upward)

    d_part, grad_gain_three = norm_back(resid_two, gain_three, nt(d_upward, w_up))
    d_resid_two = flat_cotangent.astype(jnp.float32) + d_part
    branch_two = d_resid_two.astype(jnp.bfloat16)
    grad_out_cross = tn(flat_mixed_two, branch_two)
    d_mixed_two = nt(branch_two, out_cross).astype(jnp.bfloat16)
    d_query_two, d_kv_two = attend_back(
        qx_two,
        kv_two,
        mixed_two,
        d_mixed_two.reshape(pages, token_count, width),
        bias,
        2,
        width // LANES,
        512,
        1024,
    )
    d_query_two = d_query_two.reshape(rows, width)
    d_kv_two = d_kv_two.reshape(-1, 2 * width)
    grad_q_cross = tn(normed_two, d_query_two)
    grad_kv_cross = tn(page_patches, d_kv_two)
    grad_kv_cross = (
        grad_kv_cross.reshape(width, width // LANES, 2, LANES)
        .transpose(0, 2, 1, 3)
        .reshape(width, 2 * width)
    )
    grad_patches = nt(d_kv_two, kv_blocks).astype(jnp.bfloat16).reshape(pages, -1, width)
    grad_patches = exchanged(grad_patches[None], 2, 0)
    grad_patches = jnp.sum(grad_patches.astype(jnp.float32), axis=0)

    d_part, grad_gain_two = norm_back(resid_one, gain_two, nt(d_query_two, q_cross))
    d_resid_one = d_resid_two + d_part
    branch_one = d_resid_one.astype(jnp.bfloat16)
    grad_out_self = tn(mixed_one, branch_one)
    d_mixed_one = nt(branch_one, out_self).astype(jnp.bfloat16)
    d_mixed_here = exchanged(d_mixed_one.reshape(pages, token_count, width), 2, 1)
    (d_packed_here,) = attend_back(
        qx_one, packed, mixed_here, padded(d_mixed_here), None, heads, blocks, 512, 512
    )
    d_packed_here = cut(d_packed_here)
    d_packed = exchanged(d_packed_here, 1, 2).reshape(rows, 3 * width)
    grad_qkv_here = tn(
        normed_one.reshape(-1, width), d_packed_here.reshape(-1, 3 * width // count)
    )
    d_part, grad_gain_one = norm_back(flat_tokens, gain_one, nt(d_packed, qkv_blocks))
    grad_tokens = d_resid_one + d_part

    def over_page(matrix):
        return lax.psum_scatter(
            matrix.astype(jnp.bfloat16), "page", scatter_dimension=0, tiled=True
        )

    def over_both(matrix):
        return lax.psum_scatter(
            over_page(matrix), "blk", scatter_dimension=1, tiled=True
        ).astype(jnp.float32)

    qkv_part = over_page(grad_qkv_here)
    qkv_pieces = [(qkv_part, 0)] + [(shifted(qkv_part, far), -far) for far in range(1, count)]
    qkv_rows = gathered(qkv_pieces, 1)
    qkv_rows = (
        qkv_rows.reshape(-1, width // lanes, 3, lanes).transpose(0, 2, 1, 3).reshape(-1, 3 * width)
    )
    size = 3 * width // count
    grad_qkv_self = lax.dynamic_slice_in_dim(qkv_rows, place * size, size, 1).astype(jnp.float32)

    gain_sums = lax.psum((grad_gain_one, grad_gain_two, grad_gain_three), ("page", "blk"))
    return (
        output.reshape(pages, token_count, width),
        grad_tokens.reshape(pages, token_count, width),
        grad_patches,
        gain_sums[0],
        grad_qkv_self,
        over_both(grad_out_self),
        gain_sums[1],
        over_both(grad_q_cross),
        over_both(grad_kv_cross),
        over_both(grad_out_cross),
        gain_sums[2],
        over_both(grad_w_up),
        over_both(grad_w_down),
    )


def solution(mesh):
    whole = P()
    cut = P("page", "blk", None)
    matrix = P("page", "blk")
    placed = (cut, cut, matrix) + (whole,) * 10 + (cut,)
    return jax.shard_map(
        on_device,
        mesh=mesh,
        in_specs=placed,
        out_specs=(
            cut,
            cut,
            cut,
            whole,
            matrix,
            matrix,
            whole,
            matrix,
            matrix,
            matrix,
            whole,
            matrix,
            matrix,
        ),
        check_vma=False,
    )
```

```python
import functools

import jax
import jax.numpy as jnp
from jax import lax
from jax.experimental import pallas as pl
from jax.experimental.pallas import tpu as pltpu
from jax.sharding import PartitionSpec as P

HEADS = 16
HEAD_DIM = 64
LANES = 128

norm_eps = 1e-05
masked_score = -1e30


def nt(left, right):
    return lax.dot_general(
        left, right, (((1,), (1,)), ((), ())), preferred_element_type=jnp.float32
    )


def nn(left, right):
    return lax.dot_general(
        left, right, (((1,), (0,)), ((), ())), preferred_element_type=jnp.float32
    )


def tn(left, right):
    return lax.dot_general(
        left, right, (((0,), (0,)), ((), ())), preferred_element_type=jnp.float32
    )


def lane_of(shape):
    return lax.broadcasted_iota(jnp.int32, shape, len(shape) - 1)


def own_lanes(shape, head):
    lane = lane_of(shape)
    return lane < HEAD_DIM if head == 0 else lane >= HEAD_DIM


def spare_lane(shape, head):
    return lane_of(shape) - (HEAD_DIM if head == 0 else 0)


def three_parts(column):
    high = column.astype(jnp.bfloat16)
    rest = column - high.astype(jnp.float32)
    middle = rest.astype(jnp.bfloat16)
    low = (rest - middle.astype(jnp.float32)).astype(jnp.bfloat16)
    return high, middle, low


safe_score = 40.0


def forward_kernel(heads, causal, tq, tk, q_ref, k_ref, v_ref, *rest):
    if causal:
        bias_ref = None
        mixed_ref, qx_ref, kx, vx, totals, tops, reach = rest
    else:
        bias_ref, mixed_ref, qx_ref, kx, vx, totals, tops, reach = rest
    step = pl.program_id(2)
    keys = k_ref.shape[0]
    scale = HEAD_DIM ** (-0.5)

    def longest(rows):
        square = rows.astype(jnp.float32)
        square = (square * square).astype(jnp.bfloat16)
        pick = lax.broadcasted_iota(jnp.int32, (16, LANES), 0)
        own = lax.broadcasted_iota(jnp.int32, (16, LANES), 1) // HEAD_DIM == pick
        lengths = nt(own.astype(jnp.float32).astype(jnp.bfloat16), square)
        return [jnp.max(lengths[h : h + 1]) * 1.05 for h in range(heads)]

    @pl.when(step == 0)
    def _():
        turned = v_ref[...].astype(jnp.float32).T.astype(jnp.bfloat16)
        ones = jnp.ones((16, keys), jnp.bfloat16)
        k = k_ref[...]
        lengths = longest(k)
        for h in range(heads):
            vx[h, :HEAD_DIM] = turned[h * HEAD_DIM : (h + 1) * HEAD_DIM]
            vx[h, HEAD_DIM:] = ones
            filler = jnp.zeros_like(k) if causal else bias_ref[...]
            kx[h] = jnp.where(own_lanes(k.shape, h), k, filler)
            reach[h] = lengths[h]

    q = q_ref[...] * jnp.bfloat16(scale)
    q_heads = []
    for h in range(heads):
        one = (spare_lane(q.shape, h) == 0).astype(jnp.float32).astype(jnp.bfloat16)
        q_heads.append(jnp.where(own_lanes(q.shape, h), q, one))
    lengths = longest(q)
    small = lengths[0] * reach[0] < safe_score * safe_score
    if heads == 2:
        small = jnp.logical_and(small, lengths[1] * reach[1] < safe_score * safe_score)

    def scores_of(h, start, masked):
        scores = nt(kx[h, pl.ds(start, tk), :], q_heads[h])
        if masked:
            key_at = start + lax.broadcasted_iota(jnp.int32, scores.shape, 0)
            query_at = step * tq + lax.broadcasted_iota(jnp.int32, scores.shape, 1)
            scores = jnp.where(key_at <= query_at, scores, masked_score)
        return scores

    def plain_tile(j, carry, masked):
        start = pl.multiple_of(j * tk, tk)
        out = []
        for h in range(heads):
            raised = jnp.exp(scores_of(h, start, masked)).astype(jnp.bfloat16)
            out.append(carry[h] + nn(vx[h, :, pl.ds(start, tk)], raised))
        return tuple(out)

    def careful_tile(j, carry, masked):
        start = pl.multiple_of(j * tk, tk)
        out = []
        for h in range(heads):
            largest, total = carry[h]
            scores = scores_of(h, start, masked)
            new_largest = jnp.maximum(largest, jnp.max(scores, axis=0, keepdims=True))
            raised = jnp.exp(scores - new_largest).astype(jnp.bfloat16)
            part = nn(vx[h, :, pl.ds(start, tk)], raised)
            out.append((new_largest, total * jnp.exp(largest - new_largest) + part))
        return tuple(out)

    def over_tiles(tile, carry):
        if causal:
            full = step * tq // tk
            carry = lax.fori_loop(0, full, lambda j, c: tile(j, c, False), carry)
            for extra in range(max(tq // tk, 1)):
                carry = tile(full + extra, carry, True)
            return carry
        for j in range(keys // tk):
            carry = tile(j, carry, False)
        return carry

    zeros = jnp.zeros((HEAD_DIM + 16, tq), jnp.float32)

    @pl.when(small)
    def _():
        carry = over_tiles(plain_tile, (zeros,) * heads)
        for h in range(heads):
            totals[h] = carry[h]
            tops[h] = jnp.zeros((8, tq), jnp.float32)

    @pl.when(jnp.logical_not(small))
    def _():
        lowest = jnp.full((1, tq), masked_score, jnp.float32)
        carry = over_tiles(careful_tile, ((lowest, zeros),) * heads)
        for h in range(heads):
            totals[h] = carry[h][1]
            tops[h] = jnp.broadcast_to(carry[h][0], (8, tq))

    blended, columns = [], []
    for h in range(heads):
        sums = totals[h, HEAD_DIM : HEAD_DIM + 1]
        blended.append(totals[h, :HEAD_DIM] / sums)
        columns.append(-(tops[h, :1] + jnp.log(sums)))
    if heads == 1:
        blended.append(jnp.zeros_like(blended[0]))
    mixed_ref[...] = jnp.concatenate(blended, 0).T.astype(mixed_ref.dtype)
    for h in range(heads):
        turned = jnp.broadcast_to(columns[h], (LANES, tq)).T
        high, middle, low = three_parts(turned)
        place = spare_lane(q.shape, h)
        qx = jnp.where(own_lanes(q.shape, h), q, jnp.zeros_like(q))
        qx = jnp.where(place == 0, jnp.ones_like(q), qx)
        qx = jnp.where(place == 1, high, qx)
        qx = jnp.where(place == 2, middle, qx)
        qx_ref[:, h * LANES : (h + 1) * LANES] = jnp.where(place == 3, low, qx)


def backward_kernel(heads, causal, tq, tk, parts, place_ref, qx_ref, k_ref, v_ref, o_ref, *rest):
    do_refs, rest = rest[:parts], rest[parts:]
    bias_ref = None
    if causal:
        packed_ref, kx, kt, vx, dx, dqt = rest
    else:
        bias_ref, dq_ref, packed_ref, kx, kt, vx, dx, dqt = rest
    queries, keys = qx_ref.shape[0], k_ref.shape[0]
    scale = HEAD_DIM ** (-0.5)
    first = 1 if causal else 0
    count = packed_ref.shape[0]
    block = keys // count

    def relative(owner):
        return lax.rem(owner - place_ref[0] + count, count) if count > 1 else 0

    k = k_ref[...]
    v = v_ref[...]
    kt[...] = (k.astype(jnp.float32) * scale).T.astype(jnp.bfloat16)
    for h in range(heads):
        own = own_lanes(k.shape, h)
        place = spare_lane(k.shape, h)
        ones = jnp.ones_like(k)
        bias = jnp.zeros_like(k) if causal else bias_ref[...]
        kx[h] = jnp.where(own, k, jnp.where(place == 0, bias, ones))
        vx[h] = jnp.where(own, v, ones)
    for part, do_ref in enumerate(do_refs):
        do = do_ref[...]
        size = do.shape[0]
        source = lax.rem(place_ref[0] - part + parts, parts) if parts > 1 else 0
        rows = pl.ds(pl.multiple_of(source * size, size), size)
        product = do.astype(jnp.float32) * o_ref[rows, :].astype(jnp.float32)
        for h in range(heads):
            own = own_lanes(do.shape, h)
            place = spare_lane(do.shape, h)
            delta = jnp.sum(jnp.where(own, product, 0.0), axis=1, keepdims=True)
            high, middle, low = three_parts(jnp.broadcast_to(-delta, do.shape))
            value = jnp.where(own, do, jnp.zeros_like(do))
            value = jnp.where(place == 0, high, value)
            value = jnp.where(place == 1, middle, value)
            dx[h, rows, :] = jnp.where(place == 2, low, value)

    dqt[...] = jnp.zeros_like(dqt)

    def tile(i, j, masked, sums):
        q_at = pl.multiple_of(i * tq, tq)
        k_at = pl.multiple_of(j * tk, tk)
        out = []
        for h in range(heads):
            qx = qx_ref[pl.ds(q_at, tq), h * LANES : (h + 1) * LANES]
            shares = jnp.exp(nt(kx[h, pl.ds(k_at, tk), :], qx))
            if masked:
                key_at = k_at + lax.broadcasted_iota(jnp.int32, shares.shape, 0)
                query_at = q_at + lax.broadcasted_iota(jnp.int32, shares.shape, 1)
                shares = jnp.where(key_at <= query_at, shares, 0.0)
            grad = dx[h, pl.ds(q_at, tq), :]
            d_shares = nt(vx[h, pl.ds(k_at, tk), :], grad)
            d_scores = (shares * d_shares).astype(jnp.bfloat16)
            dv = nn(shares.astype(jnp.bfloat16), grad)
            dk = nn(d_scores, qx)
            rows = pl.ds(h * HEAD_DIM, HEAD_DIM)
            dqt[rows, pl.ds(q_at, tq)] += nn(kt[rows, pl.ds(k_at, tk)], d_scores)
            if sums is not None:
                dk, dv = sums[h][0] + dk, sums[h][1] + dv
            out.append((dk, dv))
        return tuple(out)

    def finish(j, sums):
        dk, dv = sums[0]
        if heads == 2:
            own = own_lanes(dk.shape, 0)
            dk, dv = jnp.where(own, dk, sums[1][0]), jnp.where(own, dv, sums[1][1])
        dk, dv = dk.astype(packed_ref.dtype), dv.astype(packed_ref.dtype)
        if count == 1:
            k_at = pl.multiple_of(j * tk, tk)
            packed_ref[0, first, pl.ds(k_at, tk), :] = dk
            packed_ref[0, first + 1, pl.ds(k_at, tk), :] = dv
        for part in range(tk // block):
            at = relative(j * (tk // block) + part)
            packed_ref[at, first] = dk[part * block : (part + 1) * block]
            packed_ref[at, first + 1] = dv[part * block : (part + 1) * block]

    if causal:

        @pl.loop(0, keys // tk)
        def _(j):
            sums = tile(j, j, True, None)
            sums = lax.fori_loop(
                j + 1, queries // tq, lambda i, s: tile(i, j, False, s), sums
            )
            finish(j, sums)

        for owner in range(count):
            turned = dqt[:, owner * block : (owner + 1) * block].T
            packed_ref[relative(owner), 0] = turned.astype(packed_ref.dtype)
    else:
        for j in range(keys // tk):
            sums = None
            for i in range(queries // tq):
                sums = tile(i, j, False, sums)
            finish(j, sums)
        dq_ref[...] = dqt[...].T.astype(dq_ref.dtype)


def tile_of(rows, largest):
    return rows if rows < largest else largest


def attend_specs(kv, causal, queries, blocks, at=0):
    keys = kv.shape[-2]
    if causal:
        kind = lambda rows, t, i: pl.BlockSpec(
            (None, None, rows, LANES), lambda p, b, *s: (p, t, s[i] if i is not None else 0, at + b)
        )
        return kind(queries, 0, 0), kind(keys, 1, None), kind(keys, 2, None)
    half = lambda at: pl.BlockSpec((None, keys, LANES), lambda p, b, *s: (p, 0, at + b))
    return None, half(0), half(blocks)


def attend(q, kv, bias, heads, blocks, tq, tk, bias_at=0):
    causal = bias is None
    pages, queries, keys = q.shape[0], q.shape[-2], kv.shape[-2]
    tq, tk = tile_of(queries, tq), tile_of(keys, tk)
    q_spec, k_spec, v_spec = attend_specs(kv, causal, tq, blocks)
    args = [q, kv, kv]
    if causal:
        in_specs = [q_spec, k_spec, v_spec]
    else:
        in_specs = [
            pl.BlockSpec((None, tq, LANES), lambda p, b, i: (p, i, b)),
            k_spec,
            v_spec,
            pl.BlockSpec((None, keys, LANES), lambda p, b, i: (p, 0, bias_at)),
        ]
        args.append(bias)
    elements = pages * blocks * heads * queries * keys // (2 if causal else 1)
    return pl.pallas_call(
        functools.partial(forward_kernel, heads, causal, tq, tk),
        grid=(pages, blocks, queries // tq),
        in_specs=in_specs,
        out_specs=[
            pl.BlockSpec((None, tq, LANES), lambda p, b, i: (p, i, b)),
            pl.BlockSpec((None, tq, heads * LANES), lambda p, b, i: (p, i, b)),
        ],
        out_shape=[
            jax.ShapeDtypeStruct((pages, queries, blocks * LANES), jnp.bfloat16),
            jax.ShapeDtypeStruct((pages, queries, blocks * heads * LANES), jnp.bfloat16),
        ],
        scratch_shapes=[
            pltpu.VMEM((heads, keys, LANES), jnp.bfloat16),
            pltpu.VMEM((heads, HEAD_DIM + 16, keys), jnp.bfloat16),
            pltpu.VMEM((heads, HEAD_DIM + 16, tq), jnp.float32),
            pltpu.VMEM((heads, 8, tq), jnp.float32),
            pltpu.SMEM((2,), jnp.float32),
        ],
        compiler_params=pltpu.CompilerParams(vmem_limit_bytes=40 << 20),
        cost_estimate=pl.CostEstimate(
            flops=elements * 40, bytes_accessed=1 << 18, transcendentals=0
        ),
        name="attend",
    )(*args)


def attend_back(
    place, qx, kv, mixed, d_mixed, bias, heads, blocks, tq, tk, count, bias_at=0, at=0
):
    causal = bias is None
    pages, queries = qx.shape[:2]
    keys = kv.shape[-2]
    tq, tk = tile_of(queries, tq), tile_of(keys, tk)
    _, k_spec, v_spec = attend_specs(kv, causal, tq, blocks, at)
    whole = lambda rows, lanes: pl.BlockSpec((None, rows, lanes), lambda p, b, s: (p, 0, b))
    read = lambda rows, lanes: pl.BlockSpec((None, rows, lanes), lambda p, b, s: (p, 0, at + b))
    in_specs = [read(queries, heads * LANES), k_spec, v_spec, read(queries, LANES)]
    in_specs += [read(part.shape[1], LANES) for part in d_mixed]
    args = [place, qx, kv, kv, mixed, *d_mixed]
    kinds = 3 if causal else 2
    out_specs = [
        pl.BlockSpec((None, count, kinds, keys // count, LANES), lambda p, b, s: (p, 0, 0, 0, b))
    ]
    out_shape = [
        jax.ShapeDtypeStruct((pages, count, kinds, keys // count, blocks * LANES), jnp.bfloat16)
    ]
    if not causal:
        in_specs.append(pl.BlockSpec((None, keys, LANES), lambda p, b, s: (p, 0, bias_at)))
        args.append(bias)
        out_specs.insert(0, whole(queries, LANES))
        out_shape.insert(0, jax.ShapeDtypeStruct((pages, queries, blocks * LANES), jnp.bfloat16))
    elements = pages * blocks * heads * queries * keys // (2 if causal else 1)
    return pl.pallas_call(
        functools.partial(backward_kernel, heads, causal, tq, tk, len(d_mixed)),
        grid_spec=pltpu.PrefetchScalarGridSpec(
            num_scalar_prefetch=1,
            grid=(pages, blocks),
            in_specs=in_specs,
            out_specs=out_specs,
            scratch_shapes=[
                pltpu.VMEM((heads, keys, LANES), jnp.bfloat16),
                pltpu.VMEM((LANES, keys), jnp.bfloat16),
                pltpu.VMEM((heads, keys, LANES), jnp.bfloat16),
                pltpu.VMEM((heads, queries, LANES), jnp.bfloat16),
                pltpu.VMEM((LANES, queries), jnp.float32),
            ],
        ),
        out_shape=out_shape,
        compiler_params=pltpu.CompilerParams(vmem_limit_bytes=40 << 20),
        cost_estimate=pl.CostEstimate(
            flops=elements * 50, bytes_accessed=1 << 18, transcendentals=0
        ),
        name="attend_back",
    )(*args)


def mean(values):
    return jnp.mean(values, axis=-1, keepdims=True)


def norm_of(values):
    center = values - mean(values)
    rstd = lax.rsqrt(mean(center * center) + norm_eps)
    return center * rstd, rstd


def norm_back(values, gain, d_normed):
    xhat, rstd = norm_of(values)
    e = d_normed * gain
    d_values = rstd * (e - mean(e) - xhat * mean(e * xhat))
    return d_values, jnp.sum(d_normed * xhat, axis=0, keepdims=True)


def row_call(kernel, name, grid, args, in_specs, outs, flops, scratch=(), aliases=None, prefetch=0):
    out_shape, out_specs = [], []
    for shape, dtype, spec in outs:
        out_shape.append(jax.ShapeDtypeStruct(shape, dtype))
        out_specs.append(spec)
    moved = sum(a.size * a.dtype.itemsize for a in args)
    return pl.pallas_call(
        kernel,
        grid_spec=pltpu.PrefetchScalarGridSpec(
            num_scalar_prefetch=prefetch,
            grid=grid,
            in_specs=in_specs,
            out_specs=out_specs,
            scratch_shapes=list(scratch),
        ),
        out_shape=out_shape,
        input_output_aliases=aliases or {},
        compiler_params=pltpu.CompilerParams(vmem_limit_bytes=48 << 20),
        cost_estimate=pl.CostEstimate(
            flops=flops // 50, bytes_accessed=moved // 50, transcendentals=0
        ),
        name=name,
    )(*args)


def fixed(*shape):
    return pl.BlockSpec(shape, lambda *_: (0,) * len(shape))


def by_rows(tile, columns):
    return pl.BlockSpec((tile, columns), lambda i, *_: (i, 0))


anywhere = pl.BlockSpec(memory_space=pl.ANY)


def enter_kernel(src_ref, x_ref, gain_ref, w_ref, *rest):
    normed_ref, packed_ref = rest[-2:]
    normed = norm_of(x_ref[...].astype(jnp.float32))[0] * gain_ref[...]
    normed = normed.astype(jnp.bfloat16)
    normed_ref[...] = normed
    packed = nn(normed, w_ref[...]).astype(jnp.bfloat16)
    for kind in range(3):
        size = packed_ref.shape[-1]
        packed_ref[kind] = packed[:, kind * size : (kind + 1) * size]


def enter(piece, source, count, gain, weight, kept):
    pages, rows, width = piece.shape
    wide = weight.shape[1] // 3
    out = [
        (
            (pages, rows * count, width),
            jnp.bfloat16,
            pl.BlockSpec((None, rows, width), lambda p, s: (p, s[0], 0)),
        ),
        (
            (pages, 3, rows * count, wide),
            jnp.bfloat16,
            pl.BlockSpec((None, 3, rows, wide), lambda p, s: (p, 0, s[0], 0)),
        ),
    ]
    args = [source, piece, gain, weight]
    specs = [
        pl.BlockSpec((None, rows, width), lambda p, s: (p, 0, 0)),
        fixed(1, width),
        fixed(width, 3 * wide),
    ]
    aliases = {}
    if kept is not None:
        args += list(kept)
        specs += [anywhere] * 2
        aliases = {4: 0, 5: 1}
    flops = 2 * pages * rows * width * 3 * wide
    return row_call(enter_kernel, "enter", (pages,), args, specs, out, flops, (), aliases, 1)


def between_kernel(parts, tile, place_ref, *refs):
    mixed_refs, refs = refs[:parts], refs[parts:]
    tokens_ref, gain_ref, out_ref, q_ref, resid_ref, normed_ref, query_ref, whole_ref = refs
    for part, mixed_ref in enumerate(mixed_refs):
        size = mixed_ref.shape[1]
        source = lax.rem(place_ref[0] - part + parts, parts) if parts > 1 else 0
        whole_ref[:, pl.ds(pl.multiple_of(source * size, size), size)] = mixed_ref[...]
    resid = tokens_ref[...].astype(jnp.float32) + nn(whole_ref[...], out_ref[...])
    resid_ref[...] = resid
    normed = (norm_of(resid)[0] * gain_ref[...]).astype(jnp.bfloat16)
    normed_ref[...] = normed
    query_ref[...] = nn(normed, q_ref[...]).astype(jnp.bfloat16)


def between(place, mixed, tokens, gain, out_weight, q_weight):
    rows, width = tokens.shape
    tile = tile_of(rows, 256)
    row = by_rows(tile, width)
    square = fixed(width, width)
    return row_call(
        functools.partial(between_kernel, len(mixed), tile),
        "between",
        (rows // tile,),
        [place, *mixed, tokens, gain, out_weight, q_weight],
        [by_rows(tile, part.shape[1]) for part in mixed]
        + [row, fixed(1, width), square, square],
        [
            ((rows, width), jnp.float32, row),
            ((rows, width), jnp.bfloat16, row),
            ((rows, width), jnp.bfloat16, row),
            ((rows, width), jnp.bfloat16, row),
        ],
        4 * rows * width * width,
        prefetch=1,
    )


def expand_kernel(
    mixed_ref, resid_ref, gain_ref, out_ref, grad_ref, up_ref, down_ref,
    resid_two_ref, normed_ref, active_ref, d_upward_ref,
):
    @pl.when(pl.program_id(0) == 0)
    def _():
        resid = resid_ref[...] + nn(mixed_ref[...], out_ref[...])
        resid_two_ref[...] = resid
        normed_ref[...] = (norm_of(resid)[0] * gain_ref[...]).astype(jnp.bfloat16)

    upward = nn(normed_ref[...], up_ref[...])
    d_active = nt(grad_ref[...], down_ref[...])
    share = 0.5 * (1.0 + lax.erf(upward * (0.5**0.5)))
    active_ref[...] = (upward * share).astype(active_ref.dtype)
    density = jnp.exp(-0.5 * upward * upward) * 0.3989422804014327
    d_upward_ref[...] = (d_active * (share + upward * density)).astype(d_upward_ref.dtype)


def expand(mixed, resid, gain, out_weight, grad, w_up, w_down):
    rows, width = grad.shape
    wide = w_up.shape[1]
    step = 512
    all_rows = fixed(rows, width)
    column = pl.BlockSpec((rows, step), lambda f: (0, f))
    return row_call(
        expand_kernel,
        "expand",
        (wide // step,),
        [mixed, resid, gain, out_weight, grad, w_up, w_down],
        [
            all_rows,
            all_rows,
            fixed(1, width),
            fixed(width, width),
            all_rows,
            pl.BlockSpec((width, step), lambda f: (0, f)),
            pl.BlockSpec((step, width), lambda f: (f, 0)),
        ],
        [
            ((rows, width), jnp.float32, all_rows),
            ((rows, width), jnp.bfloat16, all_rows),
            ((rows, wide), jnp.bfloat16, column),
            ((rows, wide), jnp.bfloat16, column),
        ],
        4 * rows * width * wide,
    )


def contract_kernel(
    d_upward_ref, up_ref, resid_ref, grad_ref, gain_ref, out_ref,
    d_resid_ref, branch_ref, d_mixed_ref, d_gain_ref,
):
    step = pl.program_id(0)
    part = nt(d_upward_ref[...], up_ref[...])

    @pl.when(step == 0)
    def _():
        d_resid_ref[...] = part

    @pl.when(step > 0)
    def _():
        d_resid_ref[...] += part

    @pl.when(step == pl.num_programs(0) - 1)
    def _():
        d_values, d_gain_ref[...] = norm_back(resid_ref[...], gain_ref[...], d_resid_ref[...])
        d_resid = grad_ref[...].astype(jnp.float32) + d_values
        d_resid_ref[...] = d_resid
        branch = d_resid.astype(jnp.bfloat16)
        branch_ref[...] = branch
        d_mixed_ref[...] = nt(branch, out_ref[...]).astype(jnp.bfloat16)


def contract(d_upward, w_up, resid, grad, gain, out_weight):
    rows, wide = d_upward.shape
    width = resid.shape[1]
    step = 1024
    all_rows = fixed(rows, width)
    return row_call(
        contract_kernel,
        "contract",
        (wide // step,),
        [d_upward, w_up, resid, grad, gain, out_weight],
        [
            pl.BlockSpec((rows, step), lambda f: (0, f)),
            pl.BlockSpec((width, step), lambda f: (0, f)),
            all_rows,
            all_rows,
            fixed(1, width),
            fixed(width, width),
        ],
        [
            ((rows, width), jnp.float32, all_rows),
            ((rows, width), jnp.bfloat16, all_rows),
            ((rows, width), jnp.bfloat16, all_rows),
            ((1, width), jnp.float32, fixed(1, width)),
        ],
        2 * rows * width * (wide + width),
    )


def between_back_kernel(
    place_ref, d_query_ref, resid_ref, d_resid_ref, gain_ref, q_ref, out_ref,
    d_out_ref, branch_ref, d_mixed_ref, d_gain_ref,
):
    d_values, d_gain = norm_back(
        resid_ref[...], gain_ref[...], nt(d_query_ref[...], q_ref[...])
    )

    @pl.when(pl.program_id(0) == 0)
    def _():
        d_gain_ref[...] = d_gain

    @pl.when(pl.program_id(0) > 0)
    def _():
        d_gain_ref[...] += d_gain

    d_resid = d_resid_ref[...] + d_values
    d_out_ref[...] = d_resid
    branch = d_resid.astype(jnp.bfloat16)
    branch_ref[...] = branch
    count, _, size = d_mixed_ref.shape
    for far in range(count):
        owner = lax.rem(place_ref[0] + far, count)
        weight = out_ref[pl.ds(pl.multiple_of(owner * size, size), size), :]
        d_mixed_ref[far] = nt(branch, weight).astype(jnp.bfloat16)


def between_back(place, d_query, resid, d_resid, gain, q_weight, out_weight, count):
    rows, width = resid.shape
    tile = tile_of(rows, 256)
    row = by_rows(tile, width)
    square = fixed(width, width)
    size = width // count
    return row_call(
        between_back_kernel,
        "between_back",
        (rows // tile,),
        [place, d_query, resid, d_resid, gain, q_weight, out_weight],
        [row, row, row, fixed(1, width), square, square],
        [
            ((rows, width), jnp.float32, row),
            ((rows, width), jnp.bfloat16, row),
            (
                (count, rows, size),
                jnp.bfloat16,
                pl.BlockSpec((count, tile, size), lambda i, s: (0, i, 0)),
            ),
            ((1, width), jnp.float32, fixed(1, width)),
        ],
        4 * rows * width * width,
        prefetch=1,
    )


def leave_kernel(parts, blocks, place_ref, *refs):
    d_packed_refs, refs = refs[: parts * blocks], refs[parts * blocks :]
    w_ref, tokens_ref, d_resid_ref, gain_ref, grad_ref, whole = refs
    kinds = 3
    width = whole.shape[1] // kinds
    for index, d_packed_ref in enumerate(d_packed_refs):
        part, block = index % parts, index // parts
        size = d_packed_ref.shape[-1]
        source = lax.rem(place_ref[0] - part + parts, parts) if parts > 1 else 0
        for kind in range(kinds):
            at = pl.multiple_of(kind * width + (source * blocks + block) * size, size)
            whole[:, pl.ds(at, size)] = d_packed_ref[kind]
    d_normed = nt(whole[...], w_ref[...])
    tokens = tokens_ref[...].astype(jnp.float32)
    grad_ref[...] = d_resid_ref[...] + norm_back(tokens, gain_ref[...], d_normed)[0]


def leave(place, d_packed, blocks, qkv, tokens, d_resid, gain):
    pages, rows, width = tokens.shape
    tile = tile_of(rows, 256)
    row = pl.BlockSpec((None, tile, width), lambda p, i, s: (p, i, 0))
    return row_call(
        functools.partial(leave_kernel, len(d_packed) // blocks, blocks),
        "leave",
        (pages, rows // tile),
        [place, *d_packed, qkv, tokens, d_resid, gain],
        [
            pl.BlockSpec((None, 3, tile, part.shape[-1]), lambda p, i, s: (p, 0, i, 0))
            for part in d_packed
        ]
        + [fixed(width, 3 * width), row, row, fixed(1, width)],
        [((pages, rows, width), jnp.float32, row)],
        6 * pages * rows * width * width,
        [pltpu.VMEM((tile, 3 * width), jnp.bfloat16)],
        prefetch=1,
    )[0]


def turned_rows(me, left, turned, scratch, pages):
    scratch[...] = left.astype(jnp.float32).T.astype(jnp.bfloat16)
    size = scratch.shape[0] // pages
    for place in range(pages):
        odd, upper = place * 2 // pages, place % (pages // 2)
        block = jnp.bitwise_xor(upper * 2 + odd, me)
        at = pl.multiple_of(block * size, size)
        turned[place * size : (place + 1) * size] = scratch[pl.ds(at, size), :]


def grad_kernel(pages, me_ref, left_ref, right_ref, *rest):
    keep_ref, send_ref, turned, scratch = rest[-4:]

    @pl.when(pl.program_id(0) == 0)
    def _():
        turned_rows(me_ref[0], left_ref[...], turned, scratch, pages)

    total = nn(turned[...], right_ref[...]).astype(jnp.bfloat16)
    half = total.shape[0] // 2
    keep_ref[...] = total[:half]
    send_ref[...] = total[half:]


def grad_gain_kernel(pages, blocks, me_ref, left_ref, *rest):
    right_refs, (weight_ref, keep_ref, send_ref, gain_ref, turned, scratch) = (
        rest[:blocks],
        rest[blocks:],
    )

    @pl.when(pl.program_id(0) == 0)
    def _():
        turned_rows(me_ref[0], left_ref[...], turned, scratch, pages)
        gain_ref[...] = jnp.zeros_like(gain_ref)

    count, block, _ = right_refs[0].shape
    total = None
    for far in range(count):
        owner = lax.rem(me_ref[1] + far, count)
        span = pl.ds(pl.multiple_of(owner * block, block), block)
        right = jnp.concatenate([right_ref[far] for right_ref in right_refs], 1)
        part = nn(turned[:, span], right)
        total = part if total is None else total + part
    size = total.shape[0] // pages
    for place in range(pages):
        odd, upper = place * 2 // pages, place % (pages // 2)
        block = jnp.bitwise_xor(upper * 2 + odd, me_ref[0])
        rows = pl.ds(pl.multiple_of(block * size, size), size)
        terms = total[place * size : (place + 1) * size] * weight_ref[rows, :].astype(jnp.float32)
        for lane in range(0, terms.shape[1], LANES):
            gain_ref[rows, :] += terms[:, lane : lane + LANES]
    total = total.astype(jnp.bfloat16)
    half = total.shape[0] // 2
    keep_ref[...] = total[:half]
    send_ref[...] = total[half:]


def grad_with_gain(where, left, rights, weight, pages):
    depth, rows = left.shape
    count, kinds, block, lanes = rights[0].shape
    own = lanes * len(rights)
    half = pl.BlockSpec((rows // 2, own), lambda j, s: (0, j))
    return row_call(
        functools.partial(grad_gain_kernel, pages, len(rights)),
        "grad_gain",
        (kinds,),
        [where, left, *rights, weight],
        [fixed(depth, rows)]
        + [pl.BlockSpec((count, None, block, lanes), lambda j, s: (0, j, 0, 0))] * len(rights)
        + [pl.BlockSpec((rows, own), lambda j, s: (0, j))],
        [
            ((rows // 2, kinds * own), jnp.bfloat16, half),
            ((rows // 2, kinds * own), jnp.bfloat16, half),
            ((rows, LANES), jnp.float32, fixed(rows, LANES)),
        ],
        2 * depth * rows * kinds * own,
        [pltpu.VMEM((rows, depth), jnp.bfloat16)] * 2,
        None,
        1,
    )


def grad_into(kept, columns, where, left, rows, right, right_spec, tiles, tile, pages):
    depth = left.shape[0]
    right_block, right_map, out_map = right_spec
    out = [
        (
            (rows // 2, columns),
            jnp.bfloat16,
            pl.BlockSpec((rows // 2, tile), lambda j, s: (0, out_map(j, s))),
        )
    ] * 2
    args = [where, left, right]
    specs = [fixed(depth, rows), pl.BlockSpec(right_block, right_map)]
    aliases = {}
    if kept is not None:
        args += list(kept)
        specs += [anywhere] * 2
        aliases = {3: 0, 4: 1}
    return row_call(
        functools.partial(grad_kernel, pages),
        "grad",
        (tiles,),
        args,
        specs,
        out,
        2 * depth * rows * tiles * tile,
        [pltpu.VMEM((rows, depth), jnp.bfloat16)] * 2,
        aliases,
        1,
    )


def grad_up_kernel(left_ref, right_ref, out_ref, turned):
    @pl.when(pl.program_id(0) == 0)
    def _():
        turned[...] = left_ref[...].astype(jnp.float32).T.astype(jnp.bfloat16)

    total = nn(turned[...], right_ref[...]).astype(jnp.bfloat16)
    pages, rows, columns = out_ref.shape
    size = total.shape[0] // pages
    for part in range(rows // size):
        piece = total[:, part * columns : (part + 1) * columns]
        out_ref[:, part * size : (part + 1) * size, :] = piece.reshape(pages, size, columns)


def grad_down_kernel(left_ref, right_ref, kept_ref, out_ref):
    turned = left_ref[...].astype(jnp.float32).T.astype(jnp.bfloat16)
    total = nn(turned, right_ref[...]).astype(jnp.bfloat16)
    size = out_ref.shape[-1]
    for place in range(out_ref.shape[0]):
        out_ref[place] = total[:, place * size : (place + 1) * size]


def grad_wide(normed, d_upward, active, grad, count, pages):
    depth, width = normed.shape
    wide = active.shape[1]
    rows, columns = wide // pages, width // count
    subs = wide // count // columns
    shape = (count, pages, 2 * rows, columns)
    (both,) = row_call(
        grad_up_kernel,
        "grad_up",
        (count,),
        [normed, d_upward],
        [fixed(depth, width), pl.BlockSpec((depth, subs * columns), lambda j: (0, j))],
        [
            (
                shape,
                jnp.bfloat16,
                pl.BlockSpec((None, pages, rows, columns), lambda j: (j, 0, 0, 0)),
            )
        ],
        2 * depth * width * wide,
        [pltpu.VMEM((width, depth), jnp.bfloat16)],
    )
    return row_call(
        grad_down_kernel,
        "grad_down",
        (pages,),
        [active, grad, both],
        [pl.BlockSpec((depth, rows), lambda j: (0, j)), fixed(depth, width), anywhere],
        [
            (
                shape,
                jnp.bfloat16,
                pl.BlockSpec((count, None, rows, columns), lambda j: (0, j, 1, 0)),
            )
        ],
        2 * depth * width * wide,
        (),
        {2: 0},
    )[0]


def swapped(value, bit):
    pages = lax.axis_size("page")
    return lax.ppermute(value, "page", [(i, i ^ (1 << bit)) for i in range(pages)])


def added(left, right):
    return (left.astype(jnp.float32) + right.astype(jnp.float32)).astype(jnp.bfloat16)


def halved(keep, send, bit):
    return keep, swapped(send, bit)


def parted(pair, side):
    keep, got = pair
    blocks = 2 if keep.shape[0] % 256 else keep.shape[0] // 128
    shape = (blocks // 2, 2, -1, keep.shape[1]) if side == 1 else (2, blocks // 2, -1, keep.shape[1])
    axis = 1 if side == 1 else 0
    pick = lambda value, half: lax.index_in_dim(
        value.reshape(shape), half, axis, keepdims=False
    ).reshape(-1, keep.shape[1])
    return added(pick(keep, 0), pick(got, 0)), added(pick(keep, 1), pick(got, 1))


def shifted(value, shift):
    count = lax.axis_size("blk")
    return lax.ppermute(value, "blk", [(i, (i + shift) % count) for i in range(count)])


def ring_pieces(value):
    count = lax.axis_size("blk")
    pieces = [(value, 0)]
    right = left = value
    for hop in range(1, (count - 1) // 2 + 1):
        right, left = shifted(right, 1), shifted(left, -1)
        pieces += [(right, -hop), (left, hop)]
    if count % 2 == 0:
        half = value.shape[1] // 2
        if count > 1:
            top, low = shifted(right[:, :half], 1), shifted(left[:, half:], -1)
            pieces.append((jnp.concatenate([top, low], 1), count // 2))
    return pieces


def gathered(pieces, axis):
    count = lax.axis_size("blk")
    place = lax.axis_index("blk")
    size = pieces[0][0].shape[axis]
    shape = list(pieces[0][0].shape)
    shape[axis] = size * count
    whole = jnp.zeros(shape, pieces[0][0].dtype)
    for piece, far in pieces:
        whole = lax.dynamic_update_slice_in_dim(
            whole, piece, (place + far) % count * size, axis
        )
    return whole


def far_first(count):
    return sorted(range(1, count), key=lambda far: -min(far, count - far))


def exchanged(value, split, join):
    count = lax.axis_size("blk")
    place = lax.axis_index("blk")
    size = value.shape[split] // count
    take = lambda far: lax.dynamic_slice_in_dim(
        value, (place + far) % count * size, size, split
    )
    pieces = [(take(0), 0)]
    for far in far_first(count):
        pieces.append((shifted(take(far), far), -far))
    return gathered(pieces, join)


def sent_to_all(value, join):
    count = lax.axis_size("blk")
    pieces = [(value, 0)] + [(shifted(value, far), -far) for far in far_first(count)]
    return gathered(pieces, join)


def together(*values):
    return lax.optimization_barrier(values)


def on_device(
    tokens,
    patches,
    patch_mask,
    gain_one,
    qkv_self,
    out_self,
    gain_two,
    q_cross,
    kv_cross,
    out_cross,
    gain_three,
    w_up,
    w_down,
    cotangent,
):
    pages, token_count, width = tokens.shape
    count = lax.axis_size("blk")
    place = lax.axis_index("blk")
    page_devices = lax.axis_size("page")
    me = lax.axis_index("page")
    rows = pages * token_count
    here = HEADS // count
    heads = 2 if here % 2 == 0 else 1
    blocks = here // heads
    lanes = heads * HEAD_DIM
    own = here * HEAD_DIM
    swift = count == 4 and page_devices == 8 and pages == 1
    where = jnp.stack([me, place]).astype(jnp.int32)
    spot = where[1:]
    gain_one, gain_two, gain_three = (g.reshape(1, width) for g in (gain_one, gain_two, gain_three))

    def cut(value):
        if lanes == LANES:
            return value
        split = value.reshape(value.shape[:-1] + (-1, LANES))[..., :lanes]
        return split.reshape(value.shape[:-1] + (-1,))

    def padded(value):
        if lanes == LANES:
            return value
        split = value.reshape(value.shape[:-1] + (-1, lanes))
        split = jnp.pad(split, [(0, 0)] * (split.ndim - 1) + [(0, LANES - lanes)])
        return split.reshape(value.shape[:-1] + (-1,))

    def received(pieces):
        got = {0: pieces[0]}
        for far in far_first(count):
            got[far] = shifted(pieces[far], far)
        return [got[far] for far in range(count)]

    def ordered(parts, axis):
        if swift:
            return parts
        return [gathered([(part, -far) for far, part in enumerate(parts)], axis)]

    qkv_here = [
        lax.dynamic_slice_in_dim(qkv_self, kind * width + place * own, own, 1) for kind in range(3)
    ]
    qkv_here = padded(jnp.concatenate(qkv_here, 1))

    kept = None
    pieces = ring_pieces(tokens)
    for piece, far in pieces:
        source = ((place + far) % count).astype(jnp.int32).reshape(1)
        kept = enter(piece, source, count, gain_one, qkv_here, kept)
    normed_one, packed = kept
    mixed_here, qx_one = attend(packed, packed, None, heads, blocks, 1024, 512)
    mixed_pieces = [
        lax.dynamic_slice_in_dim(
            cut(mixed_here), (place + far) % count * token_count, token_count, 1
        ).reshape(rows, own)
        for far in range(count)
    ]
    mixed_parts = ordered(received(mixed_pieces), 1)

    dead = jnp.where(patch_mask > 0, 0.0, masked_score).astype(jnp.bfloat16)
    dead = jnp.broadcast_to(dead[:, :, None], dead.shape + (LANES,))
    patches_wide, _ = together(jnp.concatenate([patches, dead], 2), pieces[-1][0])
    patches_all = lax.all_gather(patches_wide, "blk", axis=1, tiled=True)
    bias_at = width // LANES
    page_patches = patches_all.reshape(-1, width + LANES)
    kv_two = nn(page_patches[:, :width], kv_cross).astype(jnp.bfloat16)
    kv_two = kv_two.reshape(pages, -1, 2 * width)

    flat_tokens = tokens.reshape(rows, width)
    resid_one, normed_two, query_two, mixed_one = between(
        spot, mixed_parts, flat_tokens, gain_two, out_self, q_cross
    )
    query_two = query_two.reshape(pages, token_count, width)
    mixed_two, qx_two = attend(
        query_two, kv_two, patches_all, 2, width // LANES, 512, 1024, bias_at
    )
    flat_mixed_two = mixed_two.reshape(rows, width)

    flat_cotangent = cotangent.reshape(rows, width)
    resid_two, normed_three, active, d_upward = expand(
        flat_mixed_two, resid_one, gain_three, out_cross, flat_cotangent, w_up, w_down
    )
    if swift:
        both = grad_wide(normed_three, d_upward, active, flat_cotangent, count, page_devices)
        d_upward, both = together(d_upward, both)
        both = lax.psum_scatter(
            both.reshape(-1, both.shape[-1]), ("blk", "page"), scatter_dimension=0, tiled=True
        ).astype(jnp.float32)

    d_resid_two, branch_two, d_mixed_two, grad_gain_three = contract(
        d_upward, w_up, resid_two, flat_cotangent, gain_three, out_cross
    )
    d_query_two, d_kv_two = attend_back(
        spot,
        qx_two,
        kv_two,
        mixed_two,
        [d_mixed_two.reshape(pages, token_count, width)],
        patches_all,
        2,
        width // LANES,
        512,
        1024,
        1,
        bias_at,
    )
    d_query_two = d_query_two.reshape(rows, width)
    d_resid_one, branch_one, d_mixed_one, grad_gain_two = between_back(
        spot, d_query_two, resid_one, d_resid_two, gain_two, q_cross, out_self, count
    )
    d_mixed_parts = ordered(
        received([d_mixed_one[far].reshape(pages, token_count, own) for far in range(count)]), 1
    )

    if swift:

        def square(at, every, depth):
            return (
                (depth, 256),
                lambda j, s: (0, lax.rem(s[1] + j, count)),
                lambda j, s: j * every + at,
            )

        def key_value(j, s):
            tile = lax.rem(s[1] + j, count)
            return (0, 0, tile // 2, 0, tile % 2)

        depth = page_patches.shape[0]
        first = grad_into(
            None,
            2 * width,
            where,
            page_patches,
            width,
            d_kv_two,
            ((None, None, None, depth, 512), key_value, lambda j, s: j),
            4,
            512,
            page_devices,
        )
        second = None
        for at, (left, right) in enumerate(
            ((flat_mixed_two, branch_two), (normed_two, d_query_two), (mixed_one, branch_one))
        ):
            second = grad_into(
                second, 3 * width, where, left, width, right, square(at, 3, rows), 4, 256, page_devices
            )
        first, second = halved(*first, 0), halved(*second, 0)
        barred = together(*d_mixed_parts, *parted(first, 1), *parted(second, 2))
        d_mixed_parts, barred = list(barred[:count]), barred[count:]
        first, second = halved(*barred[:2], 1), halved(*barred[2:], 2)

    d_packed_here, d_packed = [], []
    for block in range(blocks):
        (grads,) = attend_back(
            spot,
            qx_one,
            packed,
            mixed_here,
            [padded(part) for part in d_mixed_parts],
            None,
            heads,
            1,
            512,
            512,
            count,
            0,
            block,
        )
        grads = cut(grads)
        sent = [grads[:, far] for far in range(count)]
        if swift and block == 1:
            barred = together(grads, *d_packed_here, first[1], second[1], d_kv_two)
            grads, d_packed_here, d_kv_two = barred[0], [barred[1]], barred[4]
            first, second = (first[0], barred[2]), (second[0], barred[3])
            first, second = halved(*parted(first, 1), 2), halved(*parted(second, 1), 1)
            keep, send, gain_rows = grad_with_gain(
                where, normed_one[0], [d_packed_here[0][0], grads[0]], qkv_here, page_devices
            )
            grad_gain_one = jnp.sum(gain_rows, axis=1) / gain_one[0]
            gains = jnp.stack([grad_gain_one, grad_gain_two[0], grad_gain_three[0]])
            third = halved(keep, send, 0)
            gains_got = swapped(gains, 0)
            barred = together(*sent, *d_packed, third[1], gains_got)
            sent, d_packed = list(barred[:count]), list(barred[count : 2 * count])
            third, gains = (third[0], barred[-2]), gains + barred[-1]
        elif swift:
            barred = together(*sent, grads, *d_mixed_parts)
            sent, grads = list(barred[:count]), barred[count]
            d_mixed_parts = list(barred[count + 1 :])
        d_packed_here.append(grads)
        d_packed += ordered(received(sent), 3)
    d_key_two, d_value_two = (d_kv_two[:, 0, kind].reshape(-1, width) for kind in range(2))
    grad_patches = nt(d_key_two, kv_cross[:, :width]) + nt(d_value_two, kv_cross[:, width:])
    grad_patches = grad_patches.astype(jnp.bfloat16).reshape(pages, -1, width)
    if swift:
        grad_patches, both = together(grad_patches, both)
    grad_patches = lax.psum_scatter(grad_patches, "blk", scatter_dimension=1, tiled=True)

    grad_tokens = leave(
        spot, d_packed, blocks, qkv_self, tokens, d_resid_one.reshape(tokens.shape), gain_one
    )

    if swift:
        rows_up = both.shape[0] // 2
        grad_w_up = (
            both[:rows_up]
            .reshape(-1, width // page_devices, both.shape[1])
            .transpose(1, 0, 2)
            .reshape(width // page_devices, -1)
        )
        grad_w_down = both[rows_up:]

        for bit in (1, 2):
            keep, send = parted(third, 1)
            gains, send = together(gains, send)
            third = halved(keep, send, bit)
            gains = gains + swapped(gains, bit)
        qkv_part = added(*third)

        def piece(far):
            kv, rest = slice(far * 512, (far + 1) * 512), slice(far * 768, (far + 1) * 768)
            owner = (place + far) % count
            block = 3 * owner + (place - 3 * owner) % 4
            qkv = lax.dynamic_slice_in_dim(qkv_part, jnp.minimum(block // 4, 2) * 256, 256, 1)
            return [
                added(first[0][:, kv], first[1][:, kv]),
                added(second[0][:, rest], second[1][:, rest]),
                qkv,
            ]

        total = first[0][:, :512].astype(jnp.float32) + first[1][:, :512].astype(jnp.float32)
        rest = second[0][:, :768].astype(jnp.float32) + second[1][:, :768].astype(jnp.float32)
        total = jnp.concatenate([total, rest], 1)
        columns = jnp.zeros((qkv_part.shape[0], 4 * 256), jnp.bfloat16)
        columns = lax.dynamic_update_slice_in_dim(
            columns, piece(0)[2], (place - 3 * place) % 4 * 256, 1
        )
        pieces = together(
            gains, *d_packed[count:], *(jnp.concatenate(piece(far), 1) for far in range(1, count))
        )
        gains, pieces = pieces[0], pieces[1 + count :]
        all_gains = gains
        for far in far_first(count):
            got = shifted(pieces[far - 1], far)
            total += got[:, :1280].astype(jnp.float32)
            columns = lax.dynamic_update_slice_in_dim(
                columns, got[:, 1280:], (place - far - 3 * place) % 4 * 256, 1
            )
            all_gains += shifted(gains, far)
        gains = all_gains
        grad_kv_cross, grad_out_cross = total[:, :512], total[:, 512:768]
        grad_q_cross, grad_out_self = total[:, 768:1024], total[:, 1024:]
        grad_qkv_self = columns[:, :768].astype(jnp.float32)
    else:

        def over_rows(matrix):
            return lax.psum_scatter(
                matrix.astype(jnp.bfloat16), "page", scatter_dimension=0, tiled=True
            )

        def over_both(matrix):
            return lax.psum_scatter(
                over_rows(matrix), "blk", scatter_dimension=1, tiled=True
            ).astype(jnp.float32)

        output_patches = page_patches[:, :width]
        grad_w_up = over_both(tn(normed_three, d_upward))
        grad_w_down = over_both(tn(active, flat_cotangent))
        grad_out_cross = over_both(tn(flat_mixed_two, branch_two))
        grad_kv_cross = over_both(
            jnp.concatenate([tn(output_patches, d_key_two), tn(output_patches, d_value_two)], 1)
        )
        grad_q_cross = over_both(tn(normed_two, d_query_two))
        grad_out_self = over_both(tn(mixed_one, branch_one))
        d_packed_here = jnp.concatenate(d_packed_here, -1)
        columns = gathered([(d_packed_here[:, far], far) for far in range(count)], 2)
        columns = columns.transpose(0, 2, 1, 3).reshape(-1, 3 * own)
        grad_here = tn(normed_one.reshape(-1, width), columns)
        qkv_part = over_rows(grad_here)
        gain_rows = jnp.sum(grad_here * cut(qkv_here).astype(jnp.float32), axis=1)
        grad_gain_one = gain_rows / gain_one[0]
        gains = jnp.stack([grad_gain_one, grad_gain_two[0], grad_gain_three[0]])
        gains = lax.psum(gains, ("page", "blk"))
        qkv_rows = sent_to_all(qkv_part[None], 0)
        qkv_rows = qkv_rows.reshape(count, -1, 3, own).transpose(1, 2, 0, 3).reshape(-1, 3 * width)
        grad_qkv_self = lax.dynamic_slice_in_dim(
            qkv_rows, place * 3 * own, 3 * own, 1
        ).astype(jnp.float32)

    output = (resid_two + nn(active, w_down)).astype(jnp.bfloat16)

    return (
        output.reshape(pages, token_count, width),
        grad_tokens,
        grad_patches.astype(jnp.float32),
        gains[0],
        grad_qkv_self,
        grad_out_self,
        gains[1],
        grad_q_cross,
        grad_kv_cross,
        grad_out_cross,
        gains[2],
        grad_w_up,
        grad_w_down,
    )


def solution(mesh):
    whole = P()
    cut = P("page", "blk", None)
    matrix = P("page", "blk")
    placed = (cut, cut, matrix) + (whole,) * 10 + (cut,)
    return jax.shard_map(
        on_device,
        mesh=mesh,
        in_specs=placed,
        out_specs=(
            cut,
            cut,
            cut,
            whole,
            matrix,
            matrix,
            whole,
            matrix,
            matrix,
            matrix,
            whole,
            matrix,
            matrix,
        ),
        check_vma=False,
    )
```

```python
import functools

import jax
import jax.numpy as jnp
from jax import lax
from jax.experimental import pallas as pl
from jax.experimental.pallas import tpu as pltpu
from jax.sharding import PartitionSpec as P

HEADS = 16
HEAD_DIM = 64
LANES = 128

norm_eps = 1e-05
masked_score = -1e30


def nt(left, right):
    return lax.dot_general(
        left, right, (((1,), (1,)), ((), ())), preferred_element_type=jnp.float32
    )


def nn(left, right):
    return lax.dot_general(
        left, right, (((1,), (0,)), ((), ())), preferred_element_type=jnp.float32
    )


def tn(left, right):
    return lax.dot_general(
        left, right, (((0,), (0,)), ((), ())), preferred_element_type=jnp.float32
    )


def lane_of(shape):
    return lax.broadcasted_iota(jnp.int32, shape, len(shape) - 1)


def own_lanes(shape, head):
    lane = lane_of(shape)
    return lane < HEAD_DIM if head == 0 else lane >= HEAD_DIM


def spare_lane(shape, head):
    return lane_of(shape) - (HEAD_DIM if head == 0 else 0)


def three_parts(column):
    high = column.astype(jnp.bfloat16)
    rest = column - high.astype(jnp.float32)
    middle = rest.astype(jnp.bfloat16)
    low = (rest - middle.astype(jnp.float32)).astype(jnp.bfloat16)
    return high, middle, low


safe_score = 40.0


def forward_kernel(heads, causal, tq, tk, q_ref, k_ref, v_ref, *rest):
    if causal:
        bias_ref = None
        mixed_ref, qx_ref, kx, vx, totals, tops, reach = rest
    else:
        bias_ref, mixed_ref, qx_ref, kx, vx, totals, tops, reach = rest
    step = pl.program_id(2)
    keys = k_ref.shape[0]
    scale = HEAD_DIM ** (-0.5)

    def longest(rows):
        square = rows.astype(jnp.float32)
        square = (square * square).astype(jnp.bfloat16)
        pick = lax.broadcasted_iota(jnp.int32, (16, LANES), 0)
        own = lax.broadcasted_iota(jnp.int32, (16, LANES), 1) // HEAD_DIM == pick
        lengths = nt(own.astype(jnp.float32).astype(jnp.bfloat16), square)
        return [jnp.max(lengths[h : h + 1]) * 1.05 for h in range(heads)]

    @pl.when(step == 0)
    def _():
        turned = v_ref[...].astype(jnp.float32).T.astype(jnp.bfloat16)
        ones = jnp.ones((16, keys), jnp.bfloat16)
        k = k_ref[...]
        lengths = longest(k)
        for h in range(heads):
            vx[h, :HEAD_DIM] = turned[h * HEAD_DIM : (h + 1) * HEAD_DIM]
            vx[h, HEAD_DIM:] = ones
            filler = jnp.zeros_like(k) if causal else bias_ref[...]
            kx[h] = jnp.where(own_lanes(k.shape, h), k, filler)
            reach[h] = lengths[h]

    q = q_ref[...] * jnp.bfloat16(scale)
    q_heads = []
    for h in range(heads):
        one = (spare_lane(q.shape, h) == 0).astype(jnp.float32).astype(jnp.bfloat16)
        q_heads.append(jnp.where(own_lanes(q.shape, h), q, one))
    lengths = longest(q)
    small = lengths[0] * reach[0] < safe_score * safe_score
    if heads == 2:
        small = jnp.logical_and(small, lengths[1] * reach[1] < safe_score * safe_score)

    def scores_of(h, start, masked):
        scores = nt(kx[h, pl.ds(start, tk), :], q_heads[h])
        if masked:
            key_at = start + lax.broadcasted_iota(jnp.int32, scores.shape, 0)
            query_at = step * tq + lax.broadcasted_iota(jnp.int32, scores.shape, 1)
            scores = jnp.where(key_at <= query_at, scores, masked_score)
        return scores

    def plain_tile(j, carry, masked):
        start = pl.multiple_of(j * tk, tk)
        out = []
        for h in range(heads):
            raised = jnp.exp(scores_of(h, start, masked)).astype(jnp.bfloat16)
            out.append(carry[h] + nn(vx[h, :, pl.ds(start, tk)], raised))
        return tuple(out)

    def careful_tile(j, carry, masked):
        start = pl.multiple_of(j * tk, tk)
        out = []
        for h in range(heads):
            largest, total = carry[h]
            scores = scores_of(h, start, masked)
            new_largest = jnp.maximum(largest, jnp.max(scores, axis=0, keepdims=True))
            raised = jnp.exp(scores - new_largest).astype(jnp.bfloat16)
            part = nn(vx[h, :, pl.ds(start, tk)], raised)
            out.append((new_largest, total * jnp.exp(largest - new_largest) + part))
        return tuple(out)

    def over_tiles(tile, carry):
        if causal:
            full = step * tq // tk
            carry = lax.fori_loop(0, full, lambda j, c: tile(j, c, False), carry)
            for extra in range(max(tq // tk, 1)):
                carry = tile(full + extra, carry, True)
            return carry
        for j in range(keys // tk):
            carry = tile(j, carry, False)
        return carry

    zeros = jnp.zeros((HEAD_DIM + 16, tq), jnp.float32)

    @pl.when(small)
    def _():
        carry = over_tiles(plain_tile, (zeros,) * heads)
        for h in range(heads):
            totals[h] = carry[h]
            tops[h] = jnp.zeros((8, tq), jnp.float32)

    @pl.when(jnp.logical_not(small))
    def _():
        lowest = jnp.full((1, tq), masked_score, jnp.float32)
        carry = over_tiles(careful_tile, ((lowest, zeros),) * heads)
        for h in range(heads):
            totals[h] = carry[h][1]
            tops[h] = jnp.broadcast_to(carry[h][0], (8, tq))

    blended, columns = [], []
    for h in range(heads):
        sums = totals[h, HEAD_DIM : HEAD_DIM + 1]
        blended.append(totals[h, :HEAD_DIM] / sums)
        columns.append(-(tops[h, :1] + jnp.log(sums)))
    if heads == 1:
        blended.append(jnp.zeros_like(blended[0]))
    mixed_ref[...] = jnp.concatenate(blended, 0).T.astype(mixed_ref.dtype)
    row = lax.broadcasted_iota(jnp.int32, (LANES, tq), 0)
    turned = jnp.where(row >= HEAD_DIM, columns[0], columns[heads - 1]).T
    high, middle, low = three_parts(turned)
    for h in range(heads):
        place = spare_lane(q.shape, h)
        qx = jnp.where(own_lanes(q.shape, h), q, jnp.zeros_like(q))
        qx = jnp.where(place == 0, jnp.ones_like(q), qx)
        qx = jnp.where(place == 1, high, qx)
        qx = jnp.where(place == 2, middle, qx)
        qx_ref[:, h * LANES : (h + 1) * LANES] = jnp.where(place == 3, low, qx)


def backward_kernel(heads, causal, tq, tk, parts, place_ref, qx_ref, k_ref, v_ref, o_ref, *rest):
    do_refs, rest = rest[:parts], rest[parts:]
    bias_ref = None
    if causal:
        packed_ref, kx, kt, vx, dx, dqt = rest
    else:
        bias_ref, dq_ref, packed_ref, kx, kt, vx, dx, dqt = rest
    queries, keys = qx_ref.shape[0], k_ref.shape[0]
    scale = HEAD_DIM ** (-0.5)
    first = 1 if causal else 0
    count = packed_ref.shape[0]
    block = keys // count

    def relative(owner):
        return lax.rem(owner - place_ref[0] + count, count) if count > 1 else 0

    k = k_ref[...]
    v = v_ref[...]
    kt[...] = (k.astype(jnp.float32) * scale).T.astype(jnp.bfloat16)
    for h in range(heads):
        own = own_lanes(k.shape, h)
        place = spare_lane(k.shape, h)
        ones = jnp.ones_like(k)
        bias = jnp.zeros_like(k) if causal else bias_ref[...]
        kx[h] = jnp.where(own, k, jnp.where(place == 0, bias, ones))
        vx[h] = jnp.where(own, v, ones)
    for part, do_ref in enumerate(do_refs):
        do = do_ref[...]
        size = do.shape[0]
        source = lax.rem(place_ref[0] - part + parts, parts) if parts > 1 else 0
        rows = pl.ds(pl.multiple_of(source * size, size), size)
        product = do.astype(jnp.float32) * o_ref[rows, :].astype(jnp.float32)
        for h in range(heads):
            own = own_lanes(do.shape, h)
            place = spare_lane(do.shape, h)
            delta = jnp.sum(jnp.where(own, product, 0.0), axis=1, keepdims=True)
            high, middle, low = three_parts(jnp.broadcast_to(-delta, do.shape))
            value = jnp.where(own, do, jnp.zeros_like(do))
            value = jnp.where(place == 0, high, value)
            value = jnp.where(place == 1, middle, value)
            dx[h, rows, :] = jnp.where(place == 2, low, value)

    dqt[...] = jnp.zeros_like(dqt)

    def tile(i, j, masked, sums):
        q_at = pl.multiple_of(i * tq, tq)
        k_at = pl.multiple_of(j * tk, tk)
        out = []
        for h in range(heads):
            qx = qx_ref[pl.ds(q_at, tq), h * LANES : (h + 1) * LANES]
            shares = jnp.exp(nt(kx[h, pl.ds(k_at, tk), :], qx))
            if masked:
                key_at = k_at + lax.broadcasted_iota(jnp.int32, shares.shape, 0)
                query_at = q_at + lax.broadcasted_iota(jnp.int32, shares.shape, 1)
                shares = jnp.where(key_at <= query_at, shares, 0.0)
            grad = dx[h, pl.ds(q_at, tq), :]
            d_shares = nt(vx[h, pl.ds(k_at, tk), :], grad)
            d_scores = (shares * d_shares).astype(jnp.bfloat16)
            dv = nn(shares.astype(jnp.bfloat16), grad)
            dk = nn(d_scores, qx)
            rows = pl.ds(h * HEAD_DIM, HEAD_DIM)
            dqt[rows, pl.ds(q_at, tq)] += nn(kt[rows, pl.ds(k_at, tk)], d_scores)
            if sums is not None:
                dk, dv = sums[h][0] + dk, sums[h][1] + dv
            out.append((dk, dv))
        return tuple(out)

    def finish(j, sums):
        dk, dv = sums[0]
        if heads == 2:
            own = own_lanes(dk.shape, 0)
            dk, dv = jnp.where(own, dk, sums[1][0]), jnp.where(own, dv, sums[1][1])
        dk, dv = dk.astype(packed_ref.dtype), dv.astype(packed_ref.dtype)
        if count == 1:
            k_at = pl.multiple_of(j * tk, tk)
            packed_ref[0, first, pl.ds(k_at, tk), :] = dk
            packed_ref[0, first + 1, pl.ds(k_at, tk), :] = dv
        for part in range(tk // block):
            at = relative(j * (tk // block) + part)
            packed_ref[at, first] = dk[part * block : (part + 1) * block]
            packed_ref[at, first + 1] = dv[part * block : (part + 1) * block]

    if causal:

        @pl.loop(0, keys // tk)
        def _(j):
            sums = tile(j, j, True, None)
            sums = lax.fori_loop(
                j + 1, queries // tq, lambda i, s: tile(i, j, False, s), sums
            )
            finish(j, sums)

        for owner in range(count):
            turned = dqt[:, owner * block : (owner + 1) * block].T
            packed_ref[relative(owner), 0] = turned.astype(packed_ref.dtype)
    else:
        for j in range(keys // tk):
            sums = None
            for i in range(queries // tq):
                sums = tile(i, j, False, sums)
            finish(j, sums)
        dq_ref[...] = dqt[...].T.astype(dq_ref.dtype)


def tile_of(rows, largest):
    return rows if rows < largest else largest


def attend_specs(kv, causal, queries, blocks, at=0):
    keys = kv.shape[-2]
    if causal:
        kind = lambda rows, t, i: pl.BlockSpec(
            (None, None, rows, LANES), lambda p, b, *s: (p, t, s[i] if i is not None else 0, at + b)
        )
        return kind(queries, 0, 0), kind(keys, 1, None), kind(keys, 2, None)
    half = lambda at: pl.BlockSpec((None, keys, LANES), lambda p, b, *s: (p, 0, at + b))
    return None, half(0), half(blocks)


def attend(q, kv, bias, heads, blocks, tq, tk, bias_at=0):
    causal = bias is None
    pages, queries, keys = q.shape[0], q.shape[-2], kv.shape[-2]
    tq, tk = tile_of(queries, tq), tile_of(keys, tk)
    q_spec, k_spec, v_spec = attend_specs(kv, causal, tq, blocks)
    args = [q, kv, kv]
    if causal:
        in_specs = [q_spec, k_spec, v_spec]
    else:
        in_specs = [
            pl.BlockSpec((None, tq, LANES), lambda p, b, i: (p, i, b)),
            k_spec,
            v_spec,
            pl.BlockSpec((None, keys, LANES), lambda p, b, i: (p, 0, bias_at)),
        ]
        args.append(bias)
    elements = pages * blocks * heads * queries * keys // (2 if causal else 1)
    return pl.pallas_call(
        functools.partial(forward_kernel, heads, causal, tq, tk),
        grid=(pages, blocks, queries // tq),
        in_specs=in_specs,
        out_specs=[
            pl.BlockSpec((None, tq, LANES), lambda p, b, i: (p, i, b)),
            pl.BlockSpec((None, tq, heads * LANES), lambda p, b, i: (p, i, b)),
        ],
        out_shape=[
            jax.ShapeDtypeStruct((pages, queries, blocks * LANES), jnp.bfloat16),
            jax.ShapeDtypeStruct((pages, queries, blocks * heads * LANES), jnp.bfloat16),
        ],
        scratch_shapes=[
            pltpu.VMEM((heads, keys, LANES), jnp.bfloat16),
            pltpu.VMEM((heads, HEAD_DIM + 16, keys), jnp.bfloat16),
            pltpu.VMEM((heads, HEAD_DIM + 16, tq), jnp.float32),
            pltpu.VMEM((heads, 8, tq), jnp.float32),
            pltpu.SMEM((2,), jnp.float32),
        ],
        compiler_params=pltpu.CompilerParams(vmem_limit_bytes=40 << 20),
        cost_estimate=pl.CostEstimate(
            flops=elements * 40, bytes_accessed=1 << 18, transcendentals=0
        ),
        name="attend",
    )(*args)


def attend_back(
    place, qx, kv, mixed, d_mixed, bias, heads, blocks, tq, tk, count, bias_at=0, at=0
):
    causal = bias is None
    pages, queries = qx.shape[:2]
    keys = kv.shape[-2]
    tq, tk = tile_of(queries, tq), tile_of(keys, tk)
    _, k_spec, v_spec = attend_specs(kv, causal, tq, blocks, at)
    whole = lambda rows, lanes: pl.BlockSpec((None, rows, lanes), lambda p, b, s: (p, 0, b))
    read = lambda rows, lanes: pl.BlockSpec((None, rows, lanes), lambda p, b, s: (p, 0, at + b))
    in_specs = [read(queries, heads * LANES), k_spec, v_spec, read(queries, LANES)]
    in_specs += [read(part.shape[1], LANES) for part in d_mixed]
    args = [place, qx, kv, kv, mixed, *d_mixed]
    kinds = 3 if causal else 2
    out_specs = [
        pl.BlockSpec((None, count, kinds, keys // count, LANES), lambda p, b, s: (p, 0, 0, 0, b))
    ]
    out_shape = [
        jax.ShapeDtypeStruct((pages, count, kinds, keys // count, blocks * LANES), jnp.bfloat16)
    ]
    if not causal:
        in_specs.append(pl.BlockSpec((None, keys, LANES), lambda p, b, s: (p, 0, bias_at)))
        args.append(bias)
        out_specs.insert(0, whole(queries, LANES))
        out_shape.insert(0, jax.ShapeDtypeStruct((pages, queries, blocks * LANES), jnp.bfloat16))
    elements = pages * blocks * heads * queries * keys // (2 if causal else 1)
    return pl.pallas_call(
        functools.partial(backward_kernel, heads, causal, tq, tk, len(d_mixed)),
        grid_spec=pltpu.PrefetchScalarGridSpec(
            num_scalar_prefetch=1,
            grid=(pages, blocks),
            in_specs=in_specs,
            out_specs=out_specs,
            scratch_shapes=[
                pltpu.VMEM((heads, keys, LANES), jnp.bfloat16),
                pltpu.VMEM((LANES, keys), jnp.bfloat16),
                pltpu.VMEM((heads, keys, LANES), jnp.bfloat16),
                pltpu.VMEM((heads, queries, LANES), jnp.bfloat16),
                pltpu.VMEM((LANES, queries), jnp.float32),
            ],
        ),
        out_shape=out_shape,
        compiler_params=pltpu.CompilerParams(vmem_limit_bytes=40 << 20),
        cost_estimate=pl.CostEstimate(
            flops=elements * 50, bytes_accessed=1 << 18, transcendentals=0
        ),
        name="attend_back",
    )(*args)


def mean(values):
    return jnp.mean(values, axis=-1, keepdims=True)


def norm_of(values):
    center = values - mean(values)
    rstd = lax.rsqrt(mean(center * center) + norm_eps)
    return center * rstd, rstd


def norm_back(values, gain, d_normed):
    xhat, rstd = norm_of(values)
    e = d_normed * gain
    d_values = rstd * (e - mean(e) - xhat * mean(e * xhat))
    return d_values, jnp.sum(d_normed * xhat, axis=0, keepdims=True)


def row_call(kernel, name, grid, args, in_specs, outs, flops, scratch=(), aliases=None, prefetch=0):
    out_shape, out_specs = [], []
    for shape, dtype, spec in outs:
        out_shape.append(jax.ShapeDtypeStruct(shape, dtype))
        out_specs.append(spec)
    moved = sum(a.size * a.dtype.itemsize for a in args)
    return pl.pallas_call(
        kernel,
        grid_spec=pltpu.PrefetchScalarGridSpec(
            num_scalar_prefetch=prefetch,
            grid=grid,
            in_specs=in_specs,
            out_specs=out_specs,
            scratch_shapes=list(scratch),
        ),
        out_shape=out_shape,
        input_output_aliases=aliases or {},
        compiler_params=pltpu.CompilerParams(vmem_limit_bytes=48 << 20),
        cost_estimate=pl.CostEstimate(
            flops=flops // 50, bytes_accessed=moved // 50, transcendentals=0
        ),
        name=name,
    )(*args)


def fixed(*shape):
    return pl.BlockSpec(shape, lambda *_: (0,) * len(shape))


def by_rows(tile, columns):
    return pl.BlockSpec((tile, columns), lambda i, *_: (i, 0))


anywhere = pl.BlockSpec(memory_space=pl.ANY)


def enter_kernel(src_ref, x_ref, gain_ref, w_ref, *rest):
    normed_ref, packed_ref = rest[-2:]
    normed = norm_of(x_ref[...].astype(jnp.float32))[0] * gain_ref[...]
    normed = normed.astype(jnp.bfloat16)
    normed_ref[...] = normed
    packed = nn(normed, w_ref[...]).astype(jnp.bfloat16)
    for kind in range(3):
        size = packed_ref.shape[-1]
        packed_ref[kind] = packed[:, kind * size : (kind + 1) * size]


def enter(piece, source, count, gain, weight, kept):
    pages, rows, width = piece.shape
    wide = weight.shape[1] // 3
    out = [
        (
            (pages, rows * count, width),
            jnp.bfloat16,
            pl.BlockSpec((None, rows, width), lambda p, s: (p, s[0], 0)),
        ),
        (
            (pages, 3, rows * count, wide),
            jnp.bfloat16,
            pl.BlockSpec((None, 3, rows, wide), lambda p, s: (p, 0, s[0], 0)),
        ),
    ]
    args = [source, piece, gain, weight]
    specs = [
        pl.BlockSpec((None, rows, width), lambda p, s: (p, 0, 0)),
        fixed(1, width),
        fixed(width, 3 * wide),
    ]
    aliases = {}
    if kept is not None:
        args += list(kept)
        specs += [anywhere] * 2
        aliases = {4: 0, 5: 1}
    flops = 2 * pages * rows * width * 3 * wide
    return row_call(enter_kernel, "enter", (pages,), args, specs, out, flops, (), aliases, 1)


def enter_cross_kernel(src_ref, x_ref, w_ref, *rest):
    whole_ref, pair_ref = rest[-2:]
    whole_ref[...] = x_ref[...]
    pair_ref[...] = nn(x_ref[:, : w_ref.shape[0]], w_ref[...]).astype(jnp.bfloat16)


def enter_cross(piece, source, count, weight, kept):
    pages, rows, wide = piece.shape
    width, both = weight.shape
    out = [
        (
            (pages, rows * count, columns),
            jnp.bfloat16,
            pl.BlockSpec((None, rows, columns), lambda p, s: (p, s[0], 0)),
        )
        for columns in (wide, both)
    ]
    args = [source, piece, weight]
    specs = [pl.BlockSpec((None, rows, wide), lambda p, s: (p, 0, 0)), fixed(width, both)]
    aliases = {}
    if kept is not None:
        args += list(kept)
        specs += [anywhere] * 2
        aliases = {3: 0, 4: 1}
    flops = 2 * pages * rows * width * both
    return row_call(
        enter_cross_kernel, "enter_cross", (pages,), args, specs, out, flops, (), aliases, 1
    )


def between_kernel(parts, tile, place_ref, *refs):
    mixed_refs, refs = refs[:parts], refs[parts:]
    tokens_ref, gain_ref, out_ref, q_ref, resid_ref, normed_ref, query_ref, whole_ref = refs
    for part, mixed_ref in enumerate(mixed_refs):
        size = mixed_ref.shape[1]
        source = lax.rem(place_ref[0] - part + parts, parts) if parts > 1 else 0
        whole_ref[:, pl.ds(pl.multiple_of(source * size, size), size)] = mixed_ref[...]
    resid = tokens_ref[...].astype(jnp.float32) + nn(whole_ref[...], out_ref[...])
    resid_ref[...] = resid
    normed = (norm_of(resid)[0] * gain_ref[...]).astype(jnp.bfloat16)
    normed_ref[...] = normed
    query_ref[...] = nn(normed, q_ref[...]).astype(jnp.bfloat16)


def between(place, mixed, tokens, gain, out_weight, q_weight):
    rows, width = tokens.shape
    tile = tile_of(rows, 256)
    row = by_rows(tile, width)
    square = fixed(width, width)
    return row_call(
        functools.partial(between_kernel, len(mixed), tile),
        "between",
        (rows // tile,),
        [place, *mixed, tokens, gain, out_weight, q_weight],
        [by_rows(tile, part.shape[1]) for part in mixed]
        + [row, fixed(1, width), square, square],
        [
            ((rows, width), jnp.float32, row),
            ((rows, width), jnp.bfloat16, row),
            ((rows, width), jnp.bfloat16, row),
            ((rows, width), jnp.bfloat16, row),
        ],
        4 * rows * width * width,
        prefetch=1,
    )


def expand_kernel(
    mixed_ref, resid_ref, gain_ref, out_ref, grad_ref, up_ref, down_ref,
    resid_two_ref, normed_ref, active_ref, d_upward_ref,
):
    @pl.when(pl.program_id(0) == 0)
    def _():
        resid = resid_ref[...] + nn(mixed_ref[...], out_ref[...])
        resid_two_ref[...] = resid
        normed_ref[...] = (norm_of(resid)[0] * gain_ref[...]).astype(jnp.bfloat16)

    upward = nn(normed_ref[...], up_ref[...])
    d_active = nt(grad_ref[...], down_ref[...])
    share = 0.5 * (1.0 + lax.erf(upward * (0.5**0.5)))
    active_ref[...] = (upward * share).astype(active_ref.dtype)
    density = jnp.exp(-0.5 * upward * upward) * 0.3989422804014327
    d_upward_ref[...] = (d_active * (share + upward * density)).astype(d_upward_ref.dtype)


def expand(mixed, resid, gain, out_weight, grad, w_up, w_down):
    rows, width = grad.shape
    wide = w_up.shape[1]
    step = 512
    all_rows = fixed(rows, width)
    column = pl.BlockSpec((rows, step), lambda f: (0, f))
    return row_call(
        expand_kernel,
        "expand",
        (wide // step,),
        [mixed, resid, gain, out_weight, grad, w_up, w_down],
        [
            all_rows,
            all_rows,
            fixed(1, width),
            fixed(width, width),
            all_rows,
            pl.BlockSpec((width, step), lambda f: (0, f)),
            pl.BlockSpec((step, width), lambda f: (f, 0)),
        ],
        [
            ((rows, width), jnp.float32, all_rows),
            ((rows, width), jnp.bfloat16, all_rows),
            ((rows, wide), jnp.bfloat16, column),
            ((rows, wide), jnp.bfloat16, column),
        ],
        4 * rows * width * wide,
    )


def contract_kernel(
    d_upward_ref, up_ref, resid_ref, grad_ref, gain_ref, out_ref,
    d_resid_ref, branch_ref, d_mixed_ref, d_gain_ref,
):
    step = pl.program_id(0)
    part = nt(d_upward_ref[...], up_ref[...])

    @pl.when(step == 0)
    def _():
        d_resid_ref[...] = part

    @pl.when(step > 0)
    def _():
        d_resid_ref[...] += part

    @pl.when(step == pl.num_programs(0) - 1)
    def _():
        d_values, d_gain_ref[...] = norm_back(resid_ref[...], gain_ref[...], d_resid_ref[...])
        d_resid = grad_ref[...].astype(jnp.float32) + d_values
        d_resid_ref[...] = d_resid
        branch = d_resid.astype(jnp.bfloat16)
        branch_ref[...] = branch
        d_mixed_ref[...] = nt(branch, out_ref[...]).astype(jnp.bfloat16)


def contract(d_upward, w_up, resid, grad, gain, out_weight):
    rows, wide = d_upward.shape
    width = resid.shape[1]
    step = 1024
    all_rows = fixed(rows, width)
    return row_call(
        contract_kernel,
        "contract",
        (wide // step,),
        [d_upward, w_up, resid, grad, gain, out_weight],
        [
            pl.BlockSpec((rows, step), lambda f: (0, f)),
            pl.BlockSpec((width, step), lambda f: (0, f)),
            all_rows,
            all_rows,
            fixed(1, width),
            fixed(width, width),
        ],
        [
            ((rows, width), jnp.float32, all_rows),
            ((rows, width), jnp.bfloat16, all_rows),
            ((rows, width), jnp.bfloat16, all_rows),
            ((1, width), jnp.float32, fixed(1, width)),
        ],
        2 * rows * width * (wide + width),
    )


def between_back_kernel(
    place_ref, d_query_ref, resid_ref, d_resid_ref, gain_ref, q_ref, out_ref,
    d_out_ref, branch_ref, d_mixed_ref, d_gain_ref,
):
    d_values, d_gain = norm_back(
        resid_ref[...], gain_ref[...], nt(d_query_ref[...], q_ref[...])
    )

    @pl.when(pl.program_id(0) == 0)
    def _():
        d_gain_ref[...] = d_gain

    @pl.when(pl.program_id(0) > 0)
    def _():
        d_gain_ref[...] += d_gain

    d_resid = d_resid_ref[...] + d_values
    d_out_ref[...] = d_resid
    branch = d_resid.astype(jnp.bfloat16)
    branch_ref[...] = branch
    count, _, size = d_mixed_ref.shape
    for far in range(count):
        owner = lax.rem(place_ref[0] + far, count)
        weight = out_ref[pl.ds(pl.multiple_of(owner * size, size), size), :]
        d_mixed_ref[far] = nt(branch, weight).astype(jnp.bfloat16)


def between_back(place, d_query, resid, d_resid, gain, q_weight, out_weight, count):
    rows, width = resid.shape
    tile = tile_of(rows, 256)
    row = by_rows(tile, width)
    square = fixed(width, width)
    size = width // count
    return row_call(
        between_back_kernel,
        "between_back",
        (rows // tile,),
        [place, d_query, resid, d_resid, gain, q_weight, out_weight],
        [row, row, row, fixed(1, width), square, square],
        [
            ((rows, width), jnp.float32, row),
            ((rows, width), jnp.bfloat16, row),
            (
                (count, rows, size),
                jnp.bfloat16,
                pl.BlockSpec((count, tile, size), lambda i, s: (0, i, 0)),
            ),
            ((1, width), jnp.float32, fixed(1, width)),
        ],
        4 * rows * width * width,
        prefetch=1,
    )


def leave_kernel(parts, blocks, place_ref, *refs):
    d_packed_refs, refs = refs[: parts * blocks], refs[parts * blocks :]
    w_ref, tokens_ref, d_resid_ref, gain_ref, grad_ref, whole = refs
    kinds = 3
    width = whole.shape[1] // kinds
    for index, d_packed_ref in enumerate(d_packed_refs):
        part, block = index % parts, index // parts
        size = d_packed_ref.shape[-1]
        source = lax.rem(place_ref[0] - part + parts, parts) if parts > 1 else 0
        for kind in range(kinds):
            at = pl.multiple_of(kind * width + (source * blocks + block) * size, size)
            whole[:, pl.ds(at, size)] = d_packed_ref[kind]
    d_normed = nt(whole[...], w_ref[...])
    tokens = tokens_ref[...].astype(jnp.float32)
    grad_ref[...] = d_resid_ref[...] + norm_back(tokens, gain_ref[...], d_normed)[0]


def leave(place, d_packed, blocks, qkv, tokens, d_resid, gain):
    pages, rows, width = tokens.shape
    tile = tile_of(rows, 256)
    row = pl.BlockSpec((None, tile, width), lambda p, i, s: (p, i, 0))
    return row_call(
        functools.partial(leave_kernel, len(d_packed) // blocks, blocks),
        "leave",
        (pages, rows // tile),
        [place, *d_packed, qkv, tokens, d_resid, gain],
        [
            pl.BlockSpec((None, 3, tile, part.shape[-1]), lambda p, i, s: (p, 0, i, 0))
            for part in d_packed
        ]
        + [fixed(width, 3 * width), row, row, fixed(1, width)],
        [((pages, rows, width), jnp.float32, row)],
        6 * pages * rows * width * width,
        [pltpu.VMEM((tile, 3 * width), jnp.bfloat16)],
        prefetch=1,
    )[0]


def turned_rows(me, left, turned, scratch, pages):
    scratch[...] = left.astype(jnp.float32).T.astype(jnp.bfloat16)
    size = scratch.shape[0] // pages
    for place in range(pages):
        odd, upper = place * 2 // pages, place % (pages // 2)
        block = jnp.bitwise_xor(upper * 2 + odd, me)
        at = pl.multiple_of(block * size, size)
        turned[place * size : (place + 1) * size] = scratch[pl.ds(at, size), :]


def grad_kernel(pages, me_ref, left_ref, right_ref, *rest):
    keep_ref, send_ref, turned, scratch = rest[-4:]

    @pl.when(pl.program_id(0) == 0)
    def _():
        turned_rows(me_ref[0], left_ref[...], turned, scratch, pages)

    total = nn(turned[...], right_ref[...]).astype(jnp.bfloat16)
    half = total.shape[0] // 2
    keep_ref[...] = total[:half]
    send_ref[...] = total[half:]


def grad_gain_kernel(pages, blocks, me_ref, left_ref, *rest):
    right_refs, (weight_ref, keep_ref, send_ref, gain_ref, turned, scratch) = (
        rest[:blocks],
        rest[blocks:],
    )

    @pl.when(pl.program_id(0) == 0)
    def _():
        turned_rows(me_ref[0], left_ref[...], turned, scratch, pages)
        gain_ref[...] = jnp.zeros_like(gain_ref)

    count, block, _ = right_refs[0].shape
    total = None
    for far in range(count):
        owner = lax.rem(me_ref[1] + far, count)
        span = pl.ds(pl.multiple_of(owner * block, block), block)
        right = jnp.concatenate([right_ref[far] for right_ref in right_refs], 1)
        part = nn(turned[:, span], right)
        total = part if total is None else total + part
    size = total.shape[0] // pages
    for place in range(pages):
        odd, upper = place * 2 // pages, place % (pages // 2)
        block = jnp.bitwise_xor(upper * 2 + odd, me_ref[0])
        rows = pl.ds(pl.multiple_of(block * size, size), size)
        terms = total[place * size : (place + 1) * size] * weight_ref[rows, :].astype(jnp.float32)
        for lane in range(0, terms.shape[1], LANES):
            gain_ref[rows, :] += terms[:, lane : lane + LANES]
    total = total.astype(jnp.bfloat16)
    half = total.shape[0] // 2
    keep_ref[...] = total[:half]
    send_ref[...] = total[half:]


def grad_with_gain(where, left, rights, weight, pages):
    depth, rows = left.shape
    count, kinds, block, lanes = rights[0].shape
    own = lanes * len(rights)
    half = pl.BlockSpec((rows // 2, own), lambda j, s: (0, j))
    return row_call(
        functools.partial(grad_gain_kernel, pages, len(rights)),
        "grad_gain",
        (kinds,),
        [where, left, *rights, weight],
        [fixed(depth, rows)]
        + [pl.BlockSpec((count, None, block, lanes), lambda j, s: (0, j, 0, 0))] * len(rights)
        + [pl.BlockSpec((rows, own), lambda j, s: (0, j))],
        [
            ((rows // 2, kinds * own), jnp.bfloat16, half),
            ((rows // 2, kinds * own), jnp.bfloat16, half),
            ((rows, LANES), jnp.float32, fixed(rows, LANES)),
        ],
        2 * depth * rows * kinds * own,
        [pltpu.VMEM((rows, depth), jnp.bfloat16)] * 2,
        None,
        1,
    )


def grad_into(kept, columns, where, left, rows, right, right_spec, tiles, tile, pages):
    depth = left.shape[0]
    right_block, right_map, out_map = right_spec
    out = [
        (
            (rows // 2, columns),
            jnp.bfloat16,
            pl.BlockSpec((rows // 2, tile), lambda j, s: (0, out_map(j, s))),
        )
    ] * 2
    args = [where, left, right]
    specs = [fixed(depth, rows), pl.BlockSpec(right_block, right_map)]
    aliases = {}
    if kept is not None:
        args += list(kept)
        specs += [anywhere] * 2
        aliases = {3: 0, 4: 1}
    return row_call(
        functools.partial(grad_kernel, pages),
        "grad",
        (tiles,),
        args,
        specs,
        out,
        2 * depth * rows * tiles * tile,
        [pltpu.VMEM((rows, depth), jnp.bfloat16)] * 2,
        aliases,
        1,
    )


def grad_up_kernel(left_ref, right_ref, out_ref, turned):
    @pl.when(pl.program_id(0) == 0)
    def _():
        turned[...] = left_ref[...].astype(jnp.float32).T.astype(jnp.bfloat16)

    total = nn(turned[...], right_ref[...]).astype(jnp.bfloat16)
    pages, rows, columns = out_ref.shape
    size = total.shape[0] // pages
    for part in range(rows // size):
        piece = total[:, part * columns : (part + 1) * columns]
        out_ref[:, part * size : (part + 1) * size, :] = piece.reshape(pages, size, columns)


def grad_down_kernel(left_ref, right_ref, kept_ref, out_ref):
    turned = left_ref[...].astype(jnp.float32).T.astype(jnp.bfloat16)
    total = nn(turned, right_ref[...]).astype(jnp.bfloat16)
    size = out_ref.shape[-1]
    for place in range(out_ref.shape[0]):
        out_ref[place] = total[:, place * size : (place + 1) * size]


def grad_wide(normed, d_upward, active, grad, count, pages):
    depth, width = normed.shape
    wide = active.shape[1]
    rows, columns = wide // pages, width // count
    subs = wide // count // columns
    shape = (count, pages, 2 * rows, columns)
    (both,) = row_call(
        grad_up_kernel,
        "grad_up",
        (count,),
        [normed, d_upward],
        [fixed(depth, width), pl.BlockSpec((depth, subs * columns), lambda j: (0, j))],
        [
            (
                shape,
                jnp.bfloat16,
                pl.BlockSpec((None, pages, rows, columns), lambda j: (j, 0, 0, 0)),
            )
        ],
        2 * depth * width * wide,
        [pltpu.VMEM((width, depth), jnp.bfloat16)],
    )
    return row_call(
        grad_down_kernel,
        "grad_down",
        (pages,),
        [active, grad, both],
        [pl.BlockSpec((depth, rows), lambda j: (0, j)), fixed(depth, width), anywhere],
        [
            (
                shape,
                jnp.bfloat16,
                pl.BlockSpec((count, None, rows, columns), lambda j: (0, j, 1, 0)),
            )
        ],
        2 * depth * width * wide,
        (),
        {2: 0},
    )[0]


def swapped(value, bit):
    pages = lax.axis_size("page")
    return lax.ppermute(value, "page", [(i, i ^ (1 << bit)) for i in range(pages)])


def added(left, right):
    return (left.astype(jnp.float32) + right.astype(jnp.float32)).astype(jnp.bfloat16)


def halved(keep, send, bit):
    return keep, swapped(send, bit)


def halved_with(keep, send, gains, bit):
    rows, columns = send.shape
    high = gains.astype(jnp.bfloat16)
    low = (gains - high.astype(jnp.float32)).astype(jnp.bfloat16)
    below = jnp.stack([high, low]).reshape(-1, columns)
    count = below.shape[0]
    below = jnp.pad(below, [(0, -count % 16), (0, 0)])
    keep, got = halved(keep, jnp.concatenate([send, below], 0), bit)
    parts = got[rows : rows + count].astype(jnp.float32).reshape(2, *gains.shape)
    return (keep, got[:rows]), high.astype(jnp.float32) + low.astype(jnp.float32) + parts[0] + parts[1]


def parted(pair, side):
    keep, got = pair
    blocks = 2 if keep.shape[0] % 256 else keep.shape[0] // 128
    shape = (blocks // 2, 2, -1, keep.shape[1]) if side == 1 else (2, blocks // 2, -1, keep.shape[1])
    axis = 1 if side == 1 else 0
    pick = lambda value, half: lax.index_in_dim(
        value.reshape(shape), half, axis, keepdims=False
    ).reshape(-1, keep.shape[1])
    return added(pick(keep, 0), pick(got, 0)), added(pick(keep, 1), pick(got, 1))


def shifted(value, shift):
    count = lax.axis_size("blk")
    return lax.ppermute(value, "blk", [(i, (i + shift) % count) for i in range(count)])


def ring_pieces(value, before_last=None):
    count = lax.axis_size("blk")
    pieces = [(value, 0)]
    right = left = value
    for hop in range(1, (count - 1) // 2 + 1):
        right, left = shifted(right, 1), shifted(left, -1)
        pieces += [(right, -hop), (left, hop)]
    if count % 2 == 0:
        half = value.shape[1] // 2
        if count > 1:
            top, low = right[:, :half], left[:, half:]
            if before_last is not None:
                top, low, _ = lax.optimization_barrier((top, low, before_last))
            top, low = shifted(top, 1), shifted(low, -1)
            pieces.append((jnp.concatenate([top, low], 1), count // 2))
    return pieces


def gathered(pieces, axis):
    count = lax.axis_size("blk")
    place = lax.axis_index("blk")
    size = pieces[0][0].shape[axis]
    shape = list(pieces[0][0].shape)
    shape[axis] = size * count
    whole = jnp.zeros(shape, pieces[0][0].dtype)
    for piece, far in pieces:
        whole = lax.dynamic_update_slice_in_dim(
            whole, piece, (place + far) % count * size, axis
        )
    return whole


def far_first(count):
    return sorted(range(1, count), key=lambda far: -min(far, count - far))


def exchanged(value, split, join):
    count = lax.axis_size("blk")
    place = lax.axis_index("blk")
    size = value.shape[split] // count
    take = lambda far: lax.dynamic_slice_in_dim(
        value, (place + far) % count * size, size, split
    )
    pieces = [(take(0), 0)]
    for far in far_first(count):
        pieces.append((shifted(take(far), far), -far))
    return gathered(pieces, join)


def sent_to_all(value, join):
    count = lax.axis_size("blk")
    pieces = [(value, 0)] + [(shifted(value, far), -far) for far in far_first(count)]
    return gathered(pieces, join)


def together(*values):
    return lax.optimization_barrier(values)


def on_device(
    tokens,
    patches,
    patch_mask,
    gain_one,
    qkv_self,
    out_self,
    gain_two,
    q_cross,
    kv_cross,
    out_cross,
    gain_three,
    w_up,
    w_down,
    cotangent,
):
    pages, token_count, width = tokens.shape
    count = lax.axis_size("blk")
    place = lax.axis_index("blk")
    page_devices = lax.axis_size("page")
    me = lax.axis_index("page")
    rows = pages * token_count
    here = HEADS // count
    heads = 2 if here % 2 == 0 else 1
    blocks = here // heads
    lanes = heads * HEAD_DIM
    own = here * HEAD_DIM
    swift = count == 4 and page_devices == 8 and pages == 1
    where = jnp.stack([me, place]).astype(jnp.int32)
    spot = where[1:]
    gain_one, gain_two, gain_three = (g.reshape(1, width) for g in (gain_one, gain_two, gain_three))

    def cut(value):
        if lanes == LANES:
            return value
        split = value.reshape(value.shape[:-1] + (-1, LANES))[..., :lanes]
        return split.reshape(value.shape[:-1] + (-1,))

    def padded(value):
        if lanes == LANES:
            return value
        split = value.reshape(value.shape[:-1] + (-1, lanes))
        split = jnp.pad(split, [(0, 0)] * (split.ndim - 1) + [(0, LANES - lanes)])
        return split.reshape(value.shape[:-1] + (-1,))

    def received(pieces):
        got = {0: pieces[0]}
        for far in far_first(count):
            got[far] = shifted(pieces[far], far)
        return [got[far] for far in range(count)]

    def ordered(parts, axis):
        if swift:
            return parts
        return [gathered([(part, -far) for far, part in enumerate(parts)], axis)]

    qkv_here = [
        lax.dynamic_slice_in_dim(qkv_self, kind * width + place * own, own, 1) for kind in range(3)
    ]
    qkv_here = padded(jnp.concatenate(qkv_here, 1))

    kept = None
    pieces = ring_pieces(tokens)
    for piece, far in pieces:
        source = ((place + far) % count).astype(jnp.int32).reshape(1)
        kept = enter(piece, source, count, gain_one, qkv_here, kept)
    normed_one, packed = kept
    mixed_here, qx_one = attend(packed, packed, None, heads, blocks, 1024, 512)
    mixed_pieces = [
        lax.dynamic_slice_in_dim(
            cut(mixed_here), (place + far) % count * token_count, token_count, 1
        ).reshape(rows, own)
        for far in range(count)
    ]
    mixed_parts = ordered(received(mixed_pieces), 1)

    dead = jnp.where(patch_mask > 0, 0.0, masked_score).astype(jnp.bfloat16)
    dead = jnp.broadcast_to(dead[:, :, None], dead.shape + (LANES,))
    patches_wide, _ = together(jnp.concatenate([patches, dead], 2), pieces[-1][0])
    kept = None
    for piece, far in ring_pieces(patches_wide, mixed_here if swift else None):
        source = ((place + far) % count).astype(jnp.int32).reshape(1)
        kept = enter_cross(piece, source, count, kv_cross, kept)
    patches_all, kv_two = kept
    bias_at = width // LANES
    page_patches = patches_all.reshape(-1, width + LANES)
    if swift:
        kv_two, *mixed_parts = together(kv_two, *mixed_parts)

    flat_tokens = tokens.reshape(rows, width)
    resid_one, normed_two, query_two, mixed_one = between(
        spot, mixed_parts, flat_tokens, gain_two, out_self, q_cross
    )
    query_two = query_two.reshape(pages, token_count, width)
    mixed_two, qx_two = attend(
        query_two, kv_two, patches_all, 2, width // LANES, 512, 1024, bias_at
    )
    flat_mixed_two = mixed_two.reshape(rows, width)

    flat_cotangent = cotangent.reshape(rows, width)
    resid_two, normed_three, active, d_upward = expand(
        flat_mixed_two, resid_one, gain_three, out_cross, flat_cotangent, w_up, w_down
    )
    if swift:
        both = grad_wide(normed_three, d_upward, active, flat_cotangent, count, page_devices)
        d_upward, both = together(d_upward, both)
        both = lax.psum_scatter(
            both.reshape(-1, both.shape[-1]), ("blk", "page"), scatter_dimension=0, tiled=True
        ).astype(jnp.float32)

    d_resid_two, branch_two, d_mixed_two, grad_gain_three = contract(
        d_upward, w_up, resid_two, flat_cotangent, gain_three, out_cross
    )
    d_query_two, d_kv_two = attend_back(
        spot,
        qx_two,
        kv_two,
        mixed_two,
        [d_mixed_two.reshape(pages, token_count, width)],
        patches_all,
        2,
        width // LANES,
        512,
        1024,
        1,
        bias_at,
    )
    d_query_two = d_query_two.reshape(rows, width)
    d_resid_one, branch_one, d_mixed_one, grad_gain_two = between_back(
        spot, d_query_two, resid_one, d_resid_two, gain_two, q_cross, out_self, count
    )
    d_mixed_parts = ordered(
        received([d_mixed_one[far].reshape(pages, token_count, own) for far in range(count)]), 1
    )

    if swift:

        def square(at, every, depth):
            return (
                (depth, 256),
                lambda j, s: (0, lax.rem(s[1] + j, count)),
                lambda j, s: j * every + at,
            )

        def key_value(j, s):
            tile = lax.rem(s[1] + j, count)
            return (0, 0, tile // 2, 0, tile % 2)

        depth = page_patches.shape[0]
        first = grad_into(
            None,
            2 * width,
            where,
            page_patches,
            width,
            d_kv_two,
            ((None, None, None, depth, 512), key_value, lambda j, s: j),
            4,
            512,
            page_devices,
        )
        second = None
        for at, (left, right) in enumerate(
            ((flat_mixed_two, branch_two), (normed_two, d_query_two), (mixed_one, branch_one))
        ):
            second = grad_into(
                second, 3 * width, where, left, width, right, square(at, 3, rows), 4, 256, page_devices
            )
        output = (resid_two + nn(active, w_down)).astype(jnp.bfloat16)
        barred = together(*d_mixed_parts, *first, *second, output)
        d_mixed_parts, barred = list(barred[:count]), barred[count:]
        first, second, output = halved(*barred[:2], 0), halved(*barred[2:4], 0), barred[4]

    d_packed_here, d_packed = [], []
    for block in range(blocks):
        (grads,) = attend_back(
            spot,
            qx_one,
            packed,
            mixed_here,
            [padded(part) for part in d_mixed_parts],
            None,
            heads,
            1,
            512,
            512,
            count,
            0,
            block,
        )
        grads = cut(grads)
        sent = [grads[:, far] for far in range(count)]
        if swift and block == 1:
            barred = together(grads, *d_packed_here, first[1], second[1], d_kv_two)
            grads, d_packed_here, d_kv_two = barred[0], [barred[1]], barred[4]
            first, second = (first[0], barred[2]), (second[0], barred[3])
            first, second = halved(*parted(first, 1), 2), halved(*parted(second, 1), 1)
            keep, send, gain_rows = grad_with_gain(
                where, normed_one[0], [d_packed_here[0][0], grads[0]], qkv_here, page_devices
            )
            grad_gain_one = jnp.sum(gain_rows, axis=1) / gain_one[0]
            gains = jnp.stack([grad_gain_one, grad_gain_two[0], grad_gain_three[0]])
            third, gains = halved_with(keep, send, gains, 0)
            barred = together(*sent, *d_packed)
            sent, d_packed = list(barred[:count]), list(barred[count:])
        elif swift:
            barred = together(*sent, grads, *d_mixed_parts, first[1], second[1])
            sent, grads = list(barred[:count]), barred[count]
            d_mixed_parts = list(barred[count + 1 : 2 * count + 1])
            first, second = (first[0], barred[-2]), (second[0], barred[-1])
            first, second = halved(*parted(first, 1), 1), halved(*parted(second, 2), 2)
        d_packed_here.append(grads)
        d_packed += ordered(received(sent), 3)
    d_key_two, d_value_two = (d_kv_two[:, 0, kind].reshape(-1, width) for kind in range(2))
    grad_patches = nt(d_key_two, kv_cross[:, :width]) + nt(d_value_two, kv_cross[:, width:])
    grad_patches = grad_patches.astype(jnp.bfloat16).reshape(pages, -1, width)
    if swift:
        grad_patches, both = together(grad_patches, both)
    grad_patches = lax.psum_scatter(grad_patches, "blk", scatter_dimension=1, tiled=True)

    if swift:
        rows_up = both.shape[0] // 2
        grad_w_up = (
            both[:rows_up]
            .reshape(-1, width // page_devices, both.shape[1])
            .transpose(1, 0, 2)
            .reshape(width // page_devices, -1)
        )
        grad_w_down = both[rows_up:]

        for bit in (1, 2):
            keep, send = parted(third, 1)
            if bit == 2:
                barred = together(send, *d_packed)
                send, d_packed = barred[0], list(barred[1:])
            third, gains = halved_with(keep, send, gains, bit)
        grad_tokens = leave(
            spot, d_packed, blocks, qkv_self, tokens, d_resid_one.reshape(tokens.shape), gain_one
        )
        qkv_part = added(*third)

        def piece(far):
            kv, rest = slice(far * 512, (far + 1) * 512), slice(far * 768, (far + 1) * 768)
            owner = (place + far) % count
            block = 3 * owner + (place - 3 * owner) % 4
            qkv = lax.dynamic_slice_in_dim(qkv_part, jnp.minimum(block // 4, 2) * 256, 256, 1)
            return [
                added(first[0][:, kv], first[1][:, kv]),
                added(second[0][:, rest], second[1][:, rest]),
                qkv,
            ]

        total = first[0][:, :512].astype(jnp.float32) + first[1][:, :512].astype(jnp.float32)
        rest = second[0][:, :768].astype(jnp.float32) + second[1][:, :768].astype(jnp.float32)
        total = jnp.concatenate([total, rest], 1)
        columns = jnp.zeros((qkv_part.shape[0], 4 * 256), jnp.bfloat16)
        columns = lax.dynamic_update_slice_in_dim(
            columns, piece(0)[2], (place - 3 * place) % 4 * 256, 1
        )
        pieces = together(
            gains, *(jnp.concatenate(piece(far), 1) for far in range(1, count))
        )
        gains, pieces = pieces[0], pieces[1:]
        all_gains = gains
        for far in far_first(count):
            got = shifted(pieces[far - 1], far)
            total += got[:, :1280].astype(jnp.float32)
            columns = lax.dynamic_update_slice_in_dim(
                columns, got[:, 1280:], (place - far - 3 * place) % 4 * 256, 1
            )
            all_gains += shifted(gains, far)
        gains = all_gains
        grad_kv_cross, grad_out_cross = total[:, :512], total[:, 512:768]
        grad_q_cross, grad_out_self = total[:, 768:1024], total[:, 1024:]
        grad_qkv_self = columns[:, :768].astype(jnp.float32)
    else:

        def over_rows(matrix):
            return lax.psum_scatter(
                matrix.astype(jnp.bfloat16), "page", scatter_dimension=0, tiled=True
            )

        def over_both(matrix):
            return lax.psum_scatter(
                over_rows(matrix), "blk", scatter_dimension=1, tiled=True
            ).astype(jnp.float32)

        grad_tokens = leave(
            spot, d_packed, blocks, qkv_self, tokens, d_resid_one.reshape(tokens.shape), gain_one
        )
        output = (resid_two + nn(active, w_down)).astype(jnp.bfloat16)
        output_patches = page_patches[:, :width]
        grad_w_up = over_both(tn(normed_three, d_upward))
        grad_w_down = over_both(tn(active, flat_cotangent))
        grad_out_cross = over_both(tn(flat_mixed_two, branch_two))
        grad_kv_cross = over_both(
            jnp.concatenate([tn(output_patches, d_key_two), tn(output_patches, d_value_two)], 1)
        )
        grad_q_cross = over_both(tn(normed_two, d_query_two))
        grad_out_self = over_both(tn(mixed_one, branch_one))
        d_packed_here = jnp.concatenate(d_packed_here, -1)
        columns = gathered([(d_packed_here[:, far], far) for far in range(count)], 2)
        columns = columns.transpose(0, 2, 1, 3).reshape(-1, 3 * own)
        grad_here = tn(normed_one.reshape(-1, width), columns)
        qkv_part = over_rows(grad_here)
        gain_rows = jnp.sum(grad_here * cut(qkv_here).astype(jnp.float32), axis=1)
        grad_gain_one = gain_rows / gain_one[0]
        gains = jnp.stack([grad_gain_one, grad_gain_two[0], grad_gain_three[0]])
        gains = lax.psum(gains, ("page", "blk"))
        qkv_rows = sent_to_all(qkv_part[None], 0)
        qkv_rows = qkv_rows.reshape(count, -1, 3, own).transpose(1, 2, 0, 3).reshape(-1, 3 * width)
        grad_qkv_self = lax.dynamic_slice_in_dim(
            qkv_rows, place * 3 * own, 3 * own, 1
        ).astype(jnp.float32)

    return (
        output.reshape(pages, token_count, width),
        grad_tokens,
        grad_patches.astype(jnp.float32),
        gains[0],
        grad_qkv_self,
        grad_out_self,
        gains[1],
        grad_q_cross,
        grad_kv_cross,
        grad_out_cross,
        gains[2],
        grad_w_up,
        grad_w_down,
    )


def solution(mesh):
    whole = P()
    cut = P("page", "blk", None)
    matrix = P("page", "blk")
    placed = (cut, cut, matrix) + (whole,) * 10 + (cut,)
    return jax.shard_map(
        on_device,
        mesh=mesh,
        in_specs=placed,
        out_specs=(
            cut,
            cut,
            cut,
            whole,
            matrix,
            matrix,
            whole,
            matrix,
            matrix,
            matrix,
            whole,
            matrix,
            matrix,
        ),
        check_vma=False,
    )
```

```python
import functools

import jax
import jax.numpy as jnp
from jax import lax
from jax.experimental import pallas as pl
from jax.experimental.pallas import tpu as pltpu
from jax.sharding import PartitionSpec as P

HEADS = 16
HEAD_DIM = 64
LANES = 128

norm_eps = 1e-05
masked_score = -1e30


def nt(left, right):
    return lax.dot_general(
        left, right, (((1,), (1,)), ((), ())), preferred_element_type=jnp.float32
    )


def nn(left, right):
    return lax.dot_general(
        left, right, (((1,), (0,)), ((), ())), preferred_element_type=jnp.float32
    )


def tn(left, right):
    return lax.dot_general(
        left, right, (((0,), (0,)), ((), ())), preferred_element_type=jnp.float32
    )


def lane_of(shape):
    return lax.broadcasted_iota(jnp.int32, shape, len(shape) - 1)


def own_lanes(shape, head):
    lane = lane_of(shape)
    return lane < HEAD_DIM if head == 0 else lane >= HEAD_DIM


def spare_lane(shape, head):
    return lane_of(shape) - (HEAD_DIM if head == 0 else 0)


def three_parts(column):
    high = column.astype(jnp.bfloat16)
    rest = column - high.astype(jnp.float32)
    middle = rest.astype(jnp.bfloat16)
    low = (rest - middle.astype(jnp.float32)).astype(jnp.bfloat16)
    return high, middle, low


safe_score = 40.0


def forward_kernel(heads, causal, tq, tk, q_ref, k_ref, v_ref, *rest):
    if causal:
        bias_ref = None
        mixed_ref, qx_ref, kx, vx, totals, tops, reach = rest
    else:
        bias_ref, mixed_ref, qx_ref, kx, vx, totals, tops, reach = rest
    step = pl.program_id(2)
    keys = k_ref.shape[0]
    scale = HEAD_DIM ** (-0.5)

    def longest(rows):
        square = rows.astype(jnp.float32)
        square = (square * square).astype(jnp.bfloat16)
        pick = lax.broadcasted_iota(jnp.int32, (16, LANES), 0)
        own = lax.broadcasted_iota(jnp.int32, (16, LANES), 1) // HEAD_DIM == pick
        lengths = nt(own.astype(jnp.float32).astype(jnp.bfloat16), square)
        return [jnp.max(lengths[h : h + 1]) * 1.05 for h in range(heads)]

    @pl.when(step == 0)
    def _():
        turned = v_ref[...].astype(jnp.float32).T.astype(jnp.bfloat16)
        ones = jnp.ones((16, keys), jnp.bfloat16)
        k = k_ref[...]
        lengths = longest(k)
        for h in range(heads):
            vx[h, :HEAD_DIM] = turned[h * HEAD_DIM : (h + 1) * HEAD_DIM]
            vx[h, HEAD_DIM:] = ones
            filler = jnp.zeros_like(k) if causal else bias_ref[...]
            kx[h] = jnp.where(own_lanes(k.shape, h), k, filler)
            reach[h] = lengths[h]

    q = q_ref[...] * jnp.bfloat16(scale)
    q_heads = []
    for h in range(heads):
        one = (spare_lane(q.shape, h) == 0).astype(jnp.float32).astype(jnp.bfloat16)
        q_heads.append(jnp.where(own_lanes(q.shape, h), q, one))
    lengths = longest(q)
    small = lengths[0] * reach[0] < safe_score * safe_score
    if heads == 2:
        small = jnp.logical_and(small, lengths[1] * reach[1] < safe_score * safe_score)

    def scores_of(h, start, masked, skip):
        scores = nt(kx[h, pl.ds(start, tk), :], q_heads[h][skip:])
        if masked:
            key_at = start + lax.broadcasted_iota(jnp.int32, scores.shape, 0)
            query_at = step * tq + skip + lax.broadcasted_iota(jnp.int32, scores.shape, 1)
            scores = jnp.where(key_at <= query_at, scores, masked_score)
        return scores

    def behind(whole, part, skip):
        return jnp.concatenate([whole[:, :skip], part], 1) if skip else part

    def plain_tile(j, carry, masked, skip=0):
        start = pl.multiple_of(j * tk, tk)
        out = []
        for h in range(heads):
            raised = jnp.exp(scores_of(h, start, masked, skip)).astype(jnp.bfloat16)
            part = carry[h][:, skip:] + nn(vx[h, :, pl.ds(start, tk)], raised)
            out.append(behind(carry[h], part, skip))
        return tuple(out)

    def careful_tile(j, carry, masked, skip=0):
        start = pl.multiple_of(j * tk, tk)
        out = []
        for h in range(heads):
            largest, total = carry[h][0][:, skip:], carry[h][1][:, skip:]
            scores = scores_of(h, start, masked, skip)
            new_largest = jnp.maximum(largest, jnp.max(scores, axis=0, keepdims=True))
            raised = jnp.exp(scores - new_largest).astype(jnp.bfloat16)
            part = nn(vx[h, :, pl.ds(start, tk)], raised)
            total = total * jnp.exp(largest - new_largest) + part
            out.append(
                (behind(carry[h][0], new_largest, skip), behind(carry[h][1], total, skip))
            )
        return tuple(out)

    def over_tiles(tile, carry):
        if causal:
            full = step * tq // tk
            carry = lax.fori_loop(0, full, lambda j, c: tile(j, c, False), carry)
            for extra in range(max(tq // tk, 1)):
                carry = tile(full + extra, carry, True, extra * tk)
            return carry
        for j in range(keys // tk):
            carry = tile(j, carry, False)
        return carry

    zeros = jnp.zeros((HEAD_DIM + 16, tq), jnp.float32)

    @pl.when(small)
    def _():
        carry = over_tiles(plain_tile, (zeros,) * heads)
        for h in range(heads):
            totals[h] = carry[h]
            tops[h] = jnp.zeros((8, tq), jnp.float32)

    @pl.when(jnp.logical_not(small))
    def _():
        lowest = jnp.full((1, tq), masked_score, jnp.float32)
        carry = over_tiles(careful_tile, ((lowest, zeros),) * heads)
        for h in range(heads):
            totals[h] = carry[h][1]
            tops[h] = jnp.broadcast_to(carry[h][0], (8, tq))

    blended, columns = [], []
    for h in range(heads):
        sums = totals[h, HEAD_DIM : HEAD_DIM + 1]
        blended.append(totals[h, :HEAD_DIM] / sums)
        columns.append(-(tops[h, :1] + jnp.log(sums)))
    if heads == 1:
        blended.append(jnp.zeros_like(blended[0]))
    mixed_ref[...] = jnp.concatenate(blended, 0).T.astype(mixed_ref.dtype)
    row = lax.broadcasted_iota(jnp.int32, (LANES, tq), 0)
    turned = jnp.where(row >= HEAD_DIM, columns[0], columns[heads - 1]).T
    high, middle, low = three_parts(turned)
    for h in range(heads):
        place = spare_lane(q.shape, h)
        qx = jnp.where(own_lanes(q.shape, h), q, jnp.zeros_like(q))
        qx = jnp.where(place == 0, jnp.ones_like(q), qx)
        qx = jnp.where(place == 1, high, qx)
        qx = jnp.where(place == 2, middle, qx)
        qx_ref[:, h * LANES : (h + 1) * LANES] = jnp.where(place == 3, low, qx)


def backward_kernel(heads, causal, tq, tk, parts, place_ref, qx_ref, k_ref, v_ref, o_ref, *rest):
    do_refs, rest = rest[:parts], rest[parts:]
    bias_ref = None
    if causal:
        packed_ref, kx, kt, vx, dx, dqt = rest
    else:
        bias_ref, dq_ref, packed_ref, kx, kt, vx, dx, dqt = rest
    queries, keys = qx_ref.shape[0], k_ref.shape[0]
    scale = HEAD_DIM ** (-0.5)
    first = 1 if causal else 0
    count = packed_ref.shape[0]
    block = keys // count

    def relative(owner):
        return lax.rem(owner - place_ref[0] + count, count) if count > 1 else 0

    k = k_ref[...]
    v = v_ref[...]
    kt[...] = (k.astype(jnp.float32) * scale).T.astype(jnp.bfloat16)
    for h in range(heads):
        own = own_lanes(k.shape, h)
        place = spare_lane(k.shape, h)
        ones = jnp.ones_like(k)
        bias = jnp.zeros_like(k) if causal else bias_ref[...]
        kx[h] = jnp.where(own, k, jnp.where(place == 0, bias, ones))
        vx[h] = jnp.where(own, v, ones)
    for part, do_ref in enumerate(do_refs):
        do = do_ref[...]
        size = do.shape[0]
        source = lax.rem(place_ref[0] - part + parts, parts) if parts > 1 else 0
        rows = pl.ds(pl.multiple_of(source * size, size), size)
        product = do.astype(jnp.float32) * o_ref[rows, :].astype(jnp.float32)
        for h in range(heads):
            own = own_lanes(do.shape, h)
            place = spare_lane(do.shape, h)
            delta = jnp.sum(jnp.where(own, product, 0.0), axis=1, keepdims=True)
            high, middle, low = three_parts(jnp.broadcast_to(-delta, do.shape))
            value = jnp.where(own, do, jnp.zeros_like(do))
            value = jnp.where(place == 0, high, value)
            value = jnp.where(place == 1, middle, value)
            dx[h, rows, :] = jnp.where(place == 2, low, value)

    dqt[...] = jnp.zeros_like(dqt)

    def tile_at(q_at, tq, k_at, tk, masked):
        out = []
        for h in range(heads):
            qx = qx_ref[pl.ds(q_at, tq), h * LANES : (h + 1) * LANES]
            shares = jnp.exp(nt(kx[h, pl.ds(k_at, tk), :], qx))
            if masked:
                key_at = k_at + lax.broadcasted_iota(jnp.int32, shares.shape, 0)
                query_at = q_at + lax.broadcasted_iota(jnp.int32, shares.shape, 1)
                shares = jnp.where(key_at <= query_at, shares, 0.0)
            grad = dx[h, pl.ds(q_at, tq), :]
            d_shares = nt(vx[h, pl.ds(k_at, tk), :], grad)
            d_scores = (shares * d_shares).astype(jnp.bfloat16)
            dv = nn(shares.astype(jnp.bfloat16), grad)
            dk = nn(d_scores, qx)
            rows = pl.ds(h * HEAD_DIM, HEAD_DIM)
            dqt[rows, pl.ds(q_at, tq)] += nn(kt[rows, pl.ds(k_at, tk)], d_scores)
            out.append((dk, dv))
        return out

    def tile(i, j, masked, sums):
        q_at = pl.multiple_of(i * tq, tq)
        k_at = pl.multiple_of(j * tk, tk)
        if masked and tq == tk and tk % (4 * LANES) == 0:
            half = tk // 2
            upper = tile_at(q_at, tq, k_at, half, True)
            lower = tile_at(
                pl.multiple_of(q_at + half, half), half, pl.multiple_of(k_at + half, half), half, True
            )
            return tuple(
                tuple(jnp.concatenate(pair, 0) for pair in zip(*both)) for both in zip(upper, lower)
            )
        out = tile_at(q_at, tq, k_at, tk, masked)
        if sums is not None:
            out = [(old[0] + new[0], old[1] + new[1]) for old, new in zip(sums, out)]
        return tuple(out)

    def finish(j, sums):
        dk, dv = sums[0]
        if heads == 2:
            own = own_lanes(dk.shape, 0)
            dk, dv = jnp.where(own, dk, sums[1][0]), jnp.where(own, dv, sums[1][1])
        dk, dv = dk.astype(packed_ref.dtype), dv.astype(packed_ref.dtype)
        if count == 1:
            k_at = pl.multiple_of(j * tk, tk)
            packed_ref[0, first, pl.ds(k_at, tk), :] = dk
            packed_ref[0, first + 1, pl.ds(k_at, tk), :] = dv
        for part in range(tk // block):
            at = relative(j * (tk // block) + part)
            packed_ref[at, first] = dk[part * block : (part + 1) * block]
            packed_ref[at, first + 1] = dv[part * block : (part + 1) * block]

    if causal:

        @pl.loop(0, keys // tk)
        def _(j):
            sums = tile(j, j, True, None)
            sums = lax.fori_loop(
                j + 1, queries // tq, lambda i, s: tile(i, j, False, s), sums
            )
            finish(j, sums)

        for owner in range(count):
            turned = dqt[:, owner * block : (owner + 1) * block].T
            packed_ref[relative(owner), 0] = turned.astype(packed_ref.dtype)
    else:
        for j in range(keys // tk):
            sums = None
            for i in range(queries // tq):
                sums = tile(i, j, False, sums)
            finish(j, sums)
        dq_ref[...] = dqt[...].T.astype(dq_ref.dtype)


def tile_of(rows, largest):
    return rows if rows < largest else largest


def attend_specs(kv, causal, queries, blocks, at=0):
    keys = kv.shape[-2]
    if causal:
        kind = lambda rows, t, i: pl.BlockSpec(
            (None, None, rows, LANES), lambda p, b, *s: (p, t, s[i] if i is not None else 0, at + b)
        )
        return kind(queries, 0, 0), kind(keys, 1, None), kind(keys, 2, None)
    half = lambda at: pl.BlockSpec((None, keys, LANES), lambda p, b, *s: (p, 0, at + b))
    return None, half(0), half(blocks)


def attend(q, kv, bias, heads, blocks, tq, tk, bias_at=0):
    causal = bias is None
    pages, queries, keys = q.shape[0], q.shape[-2], kv.shape[-2]
    tq, tk = tile_of(queries, tq), tile_of(keys, tk)
    q_spec, k_spec, v_spec = attend_specs(kv, causal, tq, blocks)
    args = [q, kv, kv]
    if causal:
        in_specs = [q_spec, k_spec, v_spec]
    else:
        in_specs = [
            pl.BlockSpec((None, tq, LANES), lambda p, b, i: (p, i, b)),
            k_spec,
            v_spec,
            pl.BlockSpec((None, keys, LANES), lambda p, b, i: (p, 0, bias_at)),
        ]
        args.append(bias)
    elements = pages * blocks * heads * queries * keys // (2 if causal else 1)
    return pl.pallas_call(
        functools.partial(forward_kernel, heads, causal, tq, tk),
        grid=(pages, blocks, queries // tq),
        in_specs=in_specs,
        out_specs=[
            pl.BlockSpec((None, tq, LANES), lambda p, b, i: (p, i, b)),
            pl.BlockSpec((None, tq, heads * LANES), lambda p, b, i: (p, i, b)),
        ],
        out_shape=[
            jax.ShapeDtypeStruct((pages, queries, blocks * LANES), jnp.bfloat16),
            jax.ShapeDtypeStruct((pages, queries, blocks * heads * LANES), jnp.bfloat16),
        ],
        scratch_shapes=[
            pltpu.VMEM((heads, keys, LANES), jnp.bfloat16),
            pltpu.VMEM((heads, HEAD_DIM + 16, keys), jnp.bfloat16),
            pltpu.VMEM((heads, HEAD_DIM + 16, tq), jnp.float32),
            pltpu.VMEM((heads, 8, tq), jnp.float32),
            pltpu.SMEM((2,), jnp.float32),
        ],
        compiler_params=pltpu.CompilerParams(vmem_limit_bytes=40 << 20),
        cost_estimate=pl.CostEstimate(
            flops=elements * 40, bytes_accessed=1 << 18, transcendentals=0
        ),
        name="attend",
    )(*args)


def attend_back(
    place, qx, kv, mixed, d_mixed, bias, heads, blocks, tq, tk, count, bias_at=0, at=0
):
    causal = bias is None
    pages, queries = qx.shape[:2]
    keys = kv.shape[-2]
    tq, tk = tile_of(queries, tq), tile_of(keys, tk)
    _, k_spec, v_spec = attend_specs(kv, causal, tq, blocks, at)
    whole = lambda rows, lanes: pl.BlockSpec((None, rows, lanes), lambda p, b, s: (p, 0, b))
    read = lambda rows, lanes: pl.BlockSpec((None, rows, lanes), lambda p, b, s: (p, 0, at + b))
    in_specs = [read(queries, heads * LANES), k_spec, v_spec, read(queries, LANES)]
    in_specs += [read(part.shape[1], LANES) for part in d_mixed]
    args = [place, qx, kv, kv, mixed, *d_mixed]
    kinds = 3 if causal else 2
    out_specs = [
        pl.BlockSpec((None, count, kinds, keys // count, LANES), lambda p, b, s: (p, 0, 0, 0, b))
    ]
    out_shape = [
        jax.ShapeDtypeStruct((pages, count, kinds, keys // count, blocks * LANES), jnp.bfloat16)
    ]
    if not causal:
        in_specs.append(pl.BlockSpec((None, keys, LANES), lambda p, b, s: (p, 0, bias_at)))
        args.append(bias)
        out_specs.insert(0, whole(queries, LANES))
        out_shape.insert(0, jax.ShapeDtypeStruct((pages, queries, blocks * LANES), jnp.bfloat16))
    elements = pages * blocks * heads * queries * keys // (2 if causal else 1)
    return pl.pallas_call(
        functools.partial(backward_kernel, heads, causal, tq, tk, len(d_mixed)),
        grid_spec=pltpu.PrefetchScalarGridSpec(
            num_scalar_prefetch=1,
            grid=(pages, blocks),
            in_specs=in_specs,
            out_specs=out_specs,
            scratch_shapes=[
                pltpu.VMEM((heads, keys, LANES), jnp.bfloat16),
                pltpu.VMEM((LANES, keys), jnp.bfloat16),
                pltpu.VMEM((heads, keys, LANES), jnp.bfloat16),
                pltpu.VMEM((heads, queries, LANES), jnp.bfloat16),
                pltpu.VMEM((LANES, queries), jnp.float32),
            ],
        ),
        out_shape=out_shape,
        compiler_params=pltpu.CompilerParams(vmem_limit_bytes=40 << 20),
        cost_estimate=pl.CostEstimate(
            flops=elements * 50, bytes_accessed=1 << 18, transcendentals=0
        ),
        name="attend_back",
    )(*args)


def mean(values):
    return jnp.mean(values, axis=-1, keepdims=True)


def norm_of(values):
    center = values - mean(values)
    rstd = lax.rsqrt(mean(center * center) + norm_eps)
    return center * rstd, rstd


def norm_back(values, gain, d_normed):
    xhat, rstd = norm_of(values)
    e = d_normed * gain
    d_values = rstd * (e - mean(e) - xhat * mean(e * xhat))
    return d_values, jnp.sum(d_normed * xhat, axis=0, keepdims=True)


def row_call(kernel, name, grid, args, in_specs, outs, flops, scratch=(), aliases=None, prefetch=0):
    out_shape, out_specs = [], []
    for shape, dtype, spec in outs:
        out_shape.append(jax.ShapeDtypeStruct(shape, dtype))
        out_specs.append(spec)
    moved = sum(a.size * a.dtype.itemsize for a in args)
    return pl.pallas_call(
        kernel,
        grid_spec=pltpu.PrefetchScalarGridSpec(
            num_scalar_prefetch=prefetch,
            grid=grid,
            in_specs=in_specs,
            out_specs=out_specs,
            scratch_shapes=list(scratch),
        ),
        out_shape=out_shape,
        input_output_aliases=aliases or {},
        compiler_params=pltpu.CompilerParams(vmem_limit_bytes=48 << 20),
        cost_estimate=pl.CostEstimate(
            flops=flops // 50, bytes_accessed=moved // 50, transcendentals=0
        ),
        name=name,
    )(*args)


def fixed(*shape):
    return pl.BlockSpec(shape, lambda *_: (0,) * len(shape))


def by_rows(tile, columns):
    return pl.BlockSpec((tile, columns), lambda i, *_: (i, 0))


anywhere = pl.BlockSpec(memory_space=pl.ANY)


def enter_kernel(src_ref, x_ref, gain_ref, w_ref, *rest):
    normed_ref, packed_ref = rest[-2:]
    normed = norm_of(x_ref[...].astype(jnp.float32))[0] * gain_ref[...]
    normed = normed.astype(jnp.bfloat16)
    normed_ref[...] = normed
    packed = nn(normed, w_ref[...]).astype(jnp.bfloat16)
    for kind in range(3):
        size = packed_ref.shape[-1]
        packed_ref[kind] = packed[:, kind * size : (kind + 1) * size]


def enter(piece, source, count, gain, weight, kept):
    pages, rows, width = piece.shape
    wide = weight.shape[1] // 3
    out = [
        (
            (pages, rows * count, width),
            jnp.bfloat16,
            pl.BlockSpec((None, rows, width), lambda p, s: (p, s[0], 0)),
        ),
        (
            (pages, 3, rows * count, wide),
            jnp.bfloat16,
            pl.BlockSpec((None, 3, rows, wide), lambda p, s: (p, 0, s[0], 0)),
        ),
    ]
    args = [source, piece, gain, weight]
    specs = [
        pl.BlockSpec((None, rows, width), lambda p, s: (p, 0, 0)),
        fixed(1, width),
        fixed(width, 3 * wide),
    ]
    aliases = {}
    if kept is not None:
        args += list(kept)
        specs += [anywhere] * 2
        aliases = {4: 0, 5: 1}
    flops = 2 * pages * rows * width * 3 * wide
    return row_call(enter_kernel, "enter", (pages,), args, specs, out, flops, (), aliases, 1)


def enter_cross_kernel(src_ref, x_ref, w_ref, *rest):
    whole_ref, pair_ref = rest[-2:]
    whole_ref[...] = x_ref[...]
    pair_ref[...] = nn(x_ref[:, : w_ref.shape[0]], w_ref[...]).astype(jnp.bfloat16)


def enter_cross(piece, source, count, weight, kept):
    pages, rows, wide = piece.shape
    width, both = weight.shape
    out = [
        (
            (pages, rows * count, columns),
            jnp.bfloat16,
            pl.BlockSpec((None, rows, columns), lambda p, s: (p, s[0], 0)),
        )
        for columns in (wide, both)
    ]
    args = [source, piece, weight]
    specs = [pl.BlockSpec((None, rows, wide), lambda p, s: (p, 0, 0)), fixed(width, both)]
    aliases = {}
    if kept is not None:
        args += list(kept)
        specs += [anywhere] * 2
        aliases = {3: 0, 4: 1}
    flops = 2 * pages * rows * width * both
    return row_call(
        enter_cross_kernel, "enter_cross", (pages,), args, specs, out, flops, (), aliases, 1
    )


def between_kernel(parts, tile, place_ref, *refs):
    mixed_refs, refs = refs[:parts], refs[parts:]
    tokens_ref, gain_ref, out_ref, q_ref, resid_ref, normed_ref, query_ref, whole_ref = refs
    for part, mixed_ref in enumerate(mixed_refs):
        size = mixed_ref.shape[1]
        source = lax.rem(place_ref[0] - part + parts, parts) if parts > 1 else 0
        whole_ref[:, pl.ds(pl.multiple_of(source * size, size), size)] = mixed_ref[...]
    resid = tokens_ref[...].astype(jnp.float32) + nn(whole_ref[...], out_ref[...])
    resid_ref[...] = resid
    normed = (norm_of(resid)[0] * gain_ref[...]).astype(jnp.bfloat16)
    normed_ref[...] = normed
    query_ref[...] = nn(normed, q_ref[...]).astype(jnp.bfloat16)


def between(place, mixed, tokens, gain, out_weight, q_weight):
    rows, width = tokens.shape
    tile = tile_of(rows, 256)
    row = by_rows(tile, width)
    square = fixed(width, width)
    return row_call(
        functools.partial(between_kernel, len(mixed), tile),
        "between",
        (rows // tile,),
        [place, *mixed, tokens, gain, out_weight, q_weight],
        [by_rows(tile, part.shape[1]) for part in mixed]
        + [row, fixed(1, width), square, square],
        [
            ((rows, width), jnp.float32, row),
            ((rows, width), jnp.bfloat16, row),
            ((rows, width), jnp.bfloat16, row),
            ((rows, width), jnp.bfloat16, row),
        ],
        4 * rows * width * width,
        prefetch=1,
    )


def expand_kernel(
    mixed_ref, resid_ref, gain_ref, out_ref, grad_ref, up_ref, down_ref,
    resid_two_ref, normed_ref, active_ref, d_upward_ref,
):
    @pl.when(pl.program_id(0) == 0)
    def _():
        resid = resid_ref[...] + nn(mixed_ref[...], out_ref[...])
        resid_two_ref[...] = resid
        normed_ref[...] = (norm_of(resid)[0] * gain_ref[...]).astype(jnp.bfloat16)

    upward = nn(normed_ref[...], up_ref[...])
    d_active = nt(grad_ref[...], down_ref[...])
    share = 0.5 * (1.0 + lax.erf(upward * (0.5**0.5)))
    active_ref[...] = (upward * share).astype(active_ref.dtype)
    density = jnp.exp(-0.5 * upward * upward) * 0.3989422804014327
    d_upward_ref[...] = (d_active * (share + upward * density)).astype(d_upward_ref.dtype)


def expand(mixed, resid, gain, out_weight, grad, w_up, w_down):
    rows, width = grad.shape
    wide = w_up.shape[1]
    step = 512
    all_rows = fixed(rows, width)
    column = pl.BlockSpec((rows, step), lambda f: (0, f))
    return row_call(
        expand_kernel,
        "expand",
        (wide // step,),
        [mixed, resid, gain, out_weight, grad, w_up, w_down],
        [
            all_rows,
            all_rows,
            fixed(1, width),
            fixed(width, width),
            all_rows,
            pl.BlockSpec((width, step), lambda f: (0, f)),
            pl.BlockSpec((step, width), lambda f: (f, 0)),
        ],
        [
            ((rows, width), jnp.float32, all_rows),
            ((rows, width), jnp.bfloat16, all_rows),
            ((rows, wide), jnp.bfloat16, column),
            ((rows, wide), jnp.bfloat16, column),
        ],
        4 * rows * width * wide,
    )


def contract_kernel(
    d_upward_ref, up_ref, resid_ref, grad_ref, gain_ref, out_ref,
    d_resid_ref, branch_ref, d_mixed_ref, d_gain_ref,
):
    step = pl.program_id(0)
    part = nt(d_upward_ref[...], up_ref[...])

    @pl.when(step == 0)
    def _():
        d_resid_ref[...] = part

    @pl.when(step > 0)
    def _():
        d_resid_ref[...] += part

    @pl.when(step == pl.num_programs(0) - 1)
    def _():
        d_values, d_gain_ref[...] = norm_back(resid_ref[...], gain_ref[...], d_resid_ref[...])
        d_resid = grad_ref[...].astype(jnp.float32) + d_values
        d_resid_ref[...] = d_resid
        branch = d_resid.astype(jnp.bfloat16)
        branch_ref[...] = branch
        d_mixed_ref[...] = nt(branch, out_ref[...]).astype(jnp.bfloat16)


def contract(d_upward, w_up, resid, grad, gain, out_weight):
    rows, wide = d_upward.shape
    width = resid.shape[1]
    step = 1024
    all_rows = fixed(rows, width)
    return row_call(
        contract_kernel,
        "contract",
        (wide // step,),
        [d_upward, w_up, resid, grad, gain, out_weight],
        [
            pl.BlockSpec((rows, step), lambda f: (0, f)),
            pl.BlockSpec((width, step), lambda f: (0, f)),
            all_rows,
            all_rows,
            fixed(1, width),
            fixed(width, width),
        ],
        [
            ((rows, width), jnp.float32, all_rows),
            ((rows, width), jnp.bfloat16, all_rows),
            ((rows, width), jnp.bfloat16, all_rows),
            ((1, width), jnp.float32, fixed(1, width)),
        ],
        2 * rows * width * (wide + width),
    )


def between_back_kernel(
    place_ref, d_query_ref, resid_ref, d_resid_ref, gain_ref, q_ref, out_ref,
    d_out_ref, branch_ref, d_mixed_ref, d_gain_ref,
):
    d_values, d_gain = norm_back(
        resid_ref[...], gain_ref[...], nt(d_query_ref[...], q_ref[...])
    )

    @pl.when(pl.program_id(0) == 0)
    def _():
        d_gain_ref[...] = d_gain

    @pl.when(pl.program_id(0) > 0)
    def _():
        d_gain_ref[...] += d_gain

    d_resid = d_resid_ref[...] + d_values
    d_out_ref[...] = d_resid
    branch = d_resid.astype(jnp.bfloat16)
    branch_ref[...] = branch
    count, _, size = d_mixed_ref.shape
    for far in range(count):
        owner = lax.rem(place_ref[0] + far, count)
        weight = out_ref[pl.ds(pl.multiple_of(owner * size, size), size), :]
        d_mixed_ref[far] = nt(branch, weight).astype(jnp.bfloat16)


def between_back(place, d_query, resid, d_resid, gain, q_weight, out_weight, count):
    rows, width = resid.shape
    tile = tile_of(rows, 256)
    row = by_rows(tile, width)
    square = fixed(width, width)
    size = width // count
    return row_call(
        between_back_kernel,
        "between_back",
        (rows // tile,),
        [place, d_query, resid, d_resid, gain, q_weight, out_weight],
        [row, row, row, fixed(1, width), square, square],
        [
            ((rows, width), jnp.float32, row),
            ((rows, width), jnp.bfloat16, row),
            (
                (count, rows, size),
                jnp.bfloat16,
                pl.BlockSpec((count, tile, size), lambda i, s: (0, i, 0)),
            ),
            ((1, width), jnp.float32, fixed(1, width)),
        ],
        4 * rows * width * width,
        prefetch=1,
    )


def leave_kernel(parts, blocks, place_ref, *refs):
    d_packed_refs, refs = refs[: parts * blocks], refs[parts * blocks :]
    w_ref, tokens_ref, d_resid_ref, gain_ref, grad_ref, whole = refs
    kinds = 3
    width = whole.shape[1] // kinds
    for index, d_packed_ref in enumerate(d_packed_refs):
        part, block = index % parts, index // parts
        size = d_packed_ref.shape[-1]
        source = lax.rem(place_ref[0] - part + parts, parts) if parts > 1 else 0
        for kind in range(kinds):
            at = pl.multiple_of(kind * width + (source * blocks + block) * size, size)
            whole[:, pl.ds(at, size)] = d_packed_ref[kind]
    d_normed = nt(whole[...], w_ref[...])
    tokens = tokens_ref[...].astype(jnp.float32)
    grad_ref[...] = d_resid_ref[...] + norm_back(tokens, gain_ref[...], d_normed)[0]


def leave(place, d_packed, blocks, qkv, tokens, d_resid, gain):
    pages, rows, width = tokens.shape
    tile = tile_of(rows, 256)
    row = pl.BlockSpec((None, tile, width), lambda p, i, s: (p, i, 0))
    return row_call(
        functools.partial(leave_kernel, len(d_packed) // blocks, blocks),
        "leave",
        (pages, rows // tile),
        [place, *d_packed, qkv, tokens, d_resid, gain],
        [
            pl.BlockSpec((None, 3, tile, part.shape[-1]), lambda p, i, s: (p, 0, i, 0))
            for part in d_packed
        ]
        + [fixed(width, 3 * width), row, row, fixed(1, width)],
        [((pages, rows, width), jnp.float32, row)],
        6 * pages * rows * width * width,
        [pltpu.VMEM((tile, 3 * width), jnp.bfloat16)],
        prefetch=1,
    )[0]


def turned_rows(me, left, turned, scratch, pages):
    scratch[...] = left.astype(jnp.float32).T.astype(jnp.bfloat16)
    size = scratch.shape[0] // pages
    for place in range(pages):
        odd, upper = place * 2 // pages, place % (pages // 2)
        block = jnp.bitwise_xor(upper * 2 + odd, me)
        at = pl.multiple_of(block * size, size)
        turned[place * size : (place + 1) * size] = scratch[pl.ds(at, size), :]


def grad_kernel(pages, me_ref, left_ref, right_ref, *rest):
    keep_ref, send_ref, turned, scratch = rest[-4:]

    @pl.when(pl.program_id(0) == 0)
    def _():
        turned_rows(me_ref[0], left_ref[...], turned, scratch, pages)

    total = nn(turned[...], right_ref[...]).astype(jnp.bfloat16)
    half = total.shape[0] // 2
    keep_ref[...] = total[:half]
    send_ref[...] = total[half:]


def grad_gain_kernel(pages, blocks, me_ref, left_ref, *rest):
    right_refs, (weight_ref, keep_ref, send_ref, gain_ref, turned, scratch) = (
        rest[:blocks],
        rest[blocks:],
    )

    @pl.when(pl.program_id(0) == 0)
    def _():
        turned_rows(me_ref[0], left_ref[...], turned, scratch, pages)
        gain_ref[...] = jnp.zeros_like(gain_ref)

    count, block, _ = right_refs[0].shape
    total = None
    for far in range(count):
        owner = lax.rem(me_ref[1] + far, count)
        span = pl.ds(pl.multiple_of(owner * block, block), block)
        right = jnp.concatenate([right_ref[far] for right_ref in right_refs], 1)
        part = nn(turned[:, span], right)
        total = part if total is None else total + part
    size = total.shape[0] // pages
    for place in range(pages):
        odd, upper = place * 2 // pages, place % (pages // 2)
        block = jnp.bitwise_xor(upper * 2 + odd, me_ref[0])
        rows = pl.ds(pl.multiple_of(block * size, size), size)
        terms = total[place * size : (place + 1) * size] * weight_ref[rows, :].astype(jnp.float32)
        for lane in range(0, terms.shape[1], LANES):
            gain_ref[rows, :] += terms[:, lane : lane + LANES]
    total = total.astype(jnp.bfloat16)
    half = total.shape[0] // 2
    keep_ref[...] = total[:half]
    send_ref[...] = total[half:]


def grad_with_gain(where, left, rights, weight, pages):
    depth, rows = left.shape
    count, kinds, block, lanes = rights[0].shape
    own = lanes * len(rights)
    half = pl.BlockSpec((rows // 2, own), lambda j, s: (0, j))
    return row_call(
        functools.partial(grad_gain_kernel, pages, len(rights)),
        "grad_gain",
        (kinds,),
        [where, left, *rights, weight],
        [fixed(depth, rows)]
        + [pl.BlockSpec((count, None, block, lanes), lambda j, s: (0, j, 0, 0))] * len(rights)
        + [pl.BlockSpec((rows, own), lambda j, s: (0, j))],
        [
            ((rows // 2, kinds * own), jnp.bfloat16, half),
            ((rows // 2, kinds * own), jnp.bfloat16, half),
            ((rows, LANES), jnp.float32, fixed(rows, LANES)),
        ],
        2 * depth * rows * kinds * own,
        [pltpu.VMEM((rows, depth), jnp.bfloat16)] * 2,
        None,
        1,
    )


def grad_into(kept, columns, where, left, rows, right, right_spec, tiles, tile, pages):
    depth = left.shape[0]
    right_block, right_map, out_map = right_spec
    out = [
        (
            (rows // 2, columns),
            jnp.bfloat16,
            pl.BlockSpec((rows // 2, tile), lambda j, s: (0, out_map(j, s))),
        )
    ] * 2
    args = [where, left, right]
    specs = [fixed(depth, rows), pl.BlockSpec(right_block, right_map)]
    aliases = {}
    if kept is not None:
        args += list(kept)
        specs += [anywhere] * 2
        aliases = {3: 0, 4: 1}
    return row_call(
        functools.partial(grad_kernel, pages),
        "grad",
        (tiles,),
        args,
        specs,
        out,
        2 * depth * rows * tiles * tile,
        [pltpu.VMEM((rows, depth), jnp.bfloat16)] * 2,
        aliases,
        1,
    )


def grad_up_kernel(left_ref, right_ref, out_ref, turned):
    @pl.when(pl.program_id(0) == 0)
    def _():
        turned[...] = left_ref[...].astype(jnp.float32).T.astype(jnp.bfloat16)

    total = nn(turned[...], right_ref[...]).astype(jnp.bfloat16)
    pages, rows, columns = out_ref.shape
    size = total.shape[0] // pages
    for part in range(rows // size):
        piece = total[:, part * columns : (part + 1) * columns]
        out_ref[:, part * size : (part + 1) * size, :] = piece.reshape(pages, size, columns)


def grad_down_kernel(left_ref, right_ref, kept_ref, out_ref):
    turned = left_ref[...].astype(jnp.float32).T.astype(jnp.bfloat16)
    total = nn(turned, right_ref[...]).astype(jnp.bfloat16)
    size = out_ref.shape[-1]
    for place in range(out_ref.shape[0]):
        out_ref[place] = total[:, place * size : (place + 1) * size]


def grad_wide(normed, d_upward, active, grad, count, pages):
    depth, width = normed.shape
    wide = active.shape[1]
    rows, columns = wide // pages, width // count
    subs = wide // count // columns
    shape = (count, pages, 2 * rows, columns)
    (both,) = row_call(
        grad_up_kernel,
        "grad_up",
        (count,),
        [normed, d_upward],
        [fixed(depth, width), pl.BlockSpec((depth, subs * columns), lambda j: (0, j))],
        [
            (
                shape,
                jnp.bfloat16,
                pl.BlockSpec((None, pages, rows, columns), lambda j: (j, 0, 0, 0)),
            )
        ],
        2 * depth * width * wide,
        [pltpu.VMEM((width, depth), jnp.bfloat16)],
    )
    return row_call(
        grad_down_kernel,
        "grad_down",
        (pages,),
        [active, grad, both],
        [pl.BlockSpec((depth, rows), lambda j: (0, j)), fixed(depth, width), anywhere],
        [
            (
                shape,
                jnp.bfloat16,
                pl.BlockSpec((count, None, rows, columns), lambda j: (0, j, 1, 0)),
            )
        ],
        2 * depth * width * wide,
        (),
        {2: 0},
    )[0]


def swapped(value, bit):
    pages = lax.axis_size("page")
    return lax.ppermute(value, "page", [(i, i ^ (1 << bit)) for i in range(pages)])


def added(left, right):
    return (left.astype(jnp.float32) + right.astype(jnp.float32)).astype(jnp.bfloat16)


def halved(keep, send, bit):
    return keep, swapped(send, bit)


def halved_with(keep, send, gains, bit):
    rows, columns = send.shape
    high = gains.astype(jnp.bfloat16)
    low = (gains - high.astype(jnp.float32)).astype(jnp.bfloat16)
    below = jnp.stack([high, low]).reshape(-1, columns)
    count = below.shape[0]
    below = jnp.pad(below, [(0, -count % 16), (0, 0)])
    keep, got = halved(keep, jnp.concatenate([send, below], 0), bit)
    parts = got[rows : rows + count].astype(jnp.float32).reshape(2, *gains.shape)
    return (keep, got[:rows]), high.astype(jnp.float32) + low.astype(jnp.float32) + parts[0] + parts[1]


def parted(pair, side):
    keep, got = pair
    blocks = 2 if keep.shape[0] % 256 else keep.shape[0] // 128
    shape = (blocks // 2, 2, -1, keep.shape[1]) if side == 1 else (2, blocks // 2, -1, keep.shape[1])
    axis = 1 if side == 1 else 0
    pick = lambda value, half: lax.index_in_dim(
        value.reshape(shape), half, axis, keepdims=False
    ).reshape(-1, keep.shape[1])
    return added(pick(keep, 0), pick(got, 0)), added(pick(keep, 1), pick(got, 1))


def shifted(value, shift):
    count = lax.axis_size("blk")
    return lax.ppermute(value, "blk", [(i, (i + shift) % count) for i in range(count)])


def ring_pieces(value, before_last=None):
    count = lax.axis_size("blk")
    pieces = [(value, 0)]
    right = left = value
    for hop in range(1, (count - 1) // 2 + 1):
        right, left = shifted(right, 1), shifted(left, -1)
        pieces += [(right, -hop), (left, hop)]
    if count % 2 == 0:
        half = value.shape[1] // 2
        if count > 1:
            top, low = right[:, :half], left[:, half:]
            if before_last is not None:
                top, low, _ = lax.optimization_barrier((top, low, before_last))
            top, low = shifted(top, 1), shifted(low, -1)
            pieces.append((jnp.concatenate([top, low], 1), count // 2))
    return pieces


def gathered(pieces, axis):
    count = lax.axis_size("blk")
    place = lax.axis_index("blk")
    size = pieces[0][0].shape[axis]
    shape = list(pieces[0][0].shape)
    shape[axis] = size * count
    whole = jnp.zeros(shape, pieces[0][0].dtype)
    for piece, far in pieces:
        whole = lax.dynamic_update_slice_in_dim(
            whole, piece, (place + far) % count * size, axis
        )
    return whole


def far_first(count):
    return sorted(range(1, count), key=lambda far: -min(far, count - far))


def exchanged(value, split, join):
    count = lax.axis_size("blk")
    place = lax.axis_index("blk")
    size = value.shape[split] // count
    take = lambda far: lax.dynamic_slice_in_dim(
        value, (place + far) % count * size, size, split
    )
    pieces = [(take(0), 0)]
    for far in far_first(count):
        pieces.append((shifted(take(far), far), -far))
    return gathered(pieces, join)


def sent_to_all(value, join):
    count = lax.axis_size("blk")
    pieces = [(value, 0)] + [(shifted(value, far), -far) for far in far_first(count)]
    return gathered(pieces, join)


def together(*values):
    return lax.optimization_barrier(values)


def on_device(
    tokens,
    patches,
    patch_mask,
    gain_one,
    qkv_self,
    out_self,
    gain_two,
    q_cross,
    kv_cross,
    out_cross,
    gain_three,
    w_up,
    w_down,
    cotangent,
):
    pages, token_count, width = tokens.shape
    count = lax.axis_size("blk")
    place = lax.axis_index("blk")
    page_devices = lax.axis_size("page")
    me = lax.axis_index("page")
    rows = pages * token_count
    here = HEADS // count
    heads = 2 if here % 2 == 0 else 1
    blocks = here // heads
    lanes = heads * HEAD_DIM
    own = here * HEAD_DIM
    swift = count == 4 and page_devices == 8 and pages == 1
    where = jnp.stack([me, place]).astype(jnp.int32)
    spot = where[1:]
    gain_one, gain_two, gain_three = (g.reshape(1, width) for g in (gain_one, gain_two, gain_three))

    def cut(value):
        if lanes == LANES:
            return value
        split = value.reshape(value.shape[:-1] + (-1, LANES))[..., :lanes]
        return split.reshape(value.shape[:-1] + (-1,))

    def padded(value):
        if lanes == LANES:
            return value
        split = value.reshape(value.shape[:-1] + (-1, lanes))
        split = jnp.pad(split, [(0, 0)] * (split.ndim - 1) + [(0, LANES - lanes)])
        return split.reshape(value.shape[:-1] + (-1,))

    def received(pieces):
        got = {0: pieces[0]}
        for far in far_first(count):
            got[far] = shifted(pieces[far], far)
        return [got[far] for far in range(count)]

    def ordered(parts, axis):
        if swift:
            return parts
        return [gathered([(part, -far) for far, part in enumerate(parts)], axis)]

    qkv_here = [
        lax.dynamic_slice_in_dim(qkv_self, kind * width + place * own, own, 1) for kind in range(3)
    ]
    qkv_here = padded(jnp.concatenate(qkv_here, 1))

    kept = None
    pieces = ring_pieces(tokens)
    for piece, far in pieces:
        source = ((place + far) % count).astype(jnp.int32).reshape(1)
        kept = enter(piece, source, count, gain_one, qkv_here, kept)
    normed_one, packed = kept
    mixed_here, qx_one = attend(packed, packed, None, heads, blocks, 2048, 512)
    mixed_pieces = [
        lax.dynamic_slice_in_dim(
            cut(mixed_here), (place + far) % count * token_count, token_count, 1
        ).reshape(rows, own)
        for far in range(count)
    ]
    mixed_parts = ordered(received(mixed_pieces), 1)

    dead = jnp.where(patch_mask > 0, 0.0, masked_score).astype(jnp.bfloat16)
    dead = jnp.broadcast_to(dead[:, :, None], dead.shape + (LANES,))
    patches_wide, _ = together(jnp.concatenate([patches, dead], 2), pieces[-1][0])
    kept = None
    for piece, far in ring_pieces(patches_wide, mixed_here if swift else None):
        source = ((place + far) % count).astype(jnp.int32).reshape(1)
        kept = enter_cross(piece, source, count, kv_cross, kept)
    patches_all, kv_two = kept
    bias_at = width // LANES
    page_patches = patches_all.reshape(-1, width + LANES)
    if swift:
        kv_two, *mixed_parts = together(kv_two, *mixed_parts)

    flat_tokens = tokens.reshape(rows, width)
    resid_one, normed_two, query_two, mixed_one = between(
        spot, mixed_parts, flat_tokens, gain_two, out_self, q_cross
    )
    query_two = query_two.reshape(pages, token_count, width)
    mixed_two, qx_two = attend(
        query_two, kv_two, patches_all, 2, width // LANES, 512, 1024, bias_at
    )
    flat_mixed_two = mixed_two.reshape(rows, width)

    flat_cotangent = cotangent.reshape(rows, width)
    resid_two, normed_three, active, d_upward = expand(
        flat_mixed_two, resid_one, gain_three, out_cross, flat_cotangent, w_up, w_down
    )
    if swift:
        both = grad_wide(normed_three, d_upward, active, flat_cotangent, count, page_devices)
        d_upward, both = together(d_upward, both)
        both = lax.psum_scatter(
            both.reshape(-1, both.shape[-1]), ("blk", "page"), scatter_dimension=0, tiled=True
        ).astype(jnp.float32)

    d_resid_two, branch_two, d_mixed_two, grad_gain_three = contract(
        d_upward, w_up, resid_two, flat_cotangent, gain_three, out_cross
    )
    d_query_two, d_kv_two = attend_back(
        spot,
        qx_two,
        kv_two,
        mixed_two,
        [d_mixed_two.reshape(pages, token_count, width)],
        patches_all,
        2,
        width // LANES,
        512,
        1024,
        1,
        bias_at,
    )
    d_query_two = d_query_two.reshape(rows, width)
    d_resid_one, branch_one, d_mixed_one, grad_gain_two = between_back(
        spot, d_query_two, resid_one, d_resid_two, gain_two, q_cross, out_self, count
    )
    d_mixed_parts = ordered(
        received([d_mixed_one[far].reshape(pages, token_count, own) for far in range(count)]), 1
    )

    if swift:

        def square(at, every, depth):
            return (
                (depth, 256),
                lambda j, s: (0, lax.rem(s[1] + j, count)),
                lambda j, s: j * every + at,
            )

        def key_value(j, s):
            tile = lax.rem(s[1] + j, count)
            return (0, 0, tile // 2, 0, tile % 2)

        depth = page_patches.shape[0]
        first = grad_into(
            None,
            2 * width,
            where,
            page_patches,
            width,
            d_kv_two,
            ((None, None, None, depth, 512), key_value, lambda j, s: j),
            4,
            512,
            page_devices,
        )
        second = None
        for at, (left, right) in enumerate(
            ((flat_mixed_two, branch_two), (normed_two, d_query_two), (mixed_one, branch_one))
        ):
            second = grad_into(
                second, 3 * width, where, left, width, right, square(at, 3, rows), 4, 256, page_devices
            )
        output = (resid_two + nn(active, w_down)).astype(jnp.bfloat16)
        barred = together(*d_mixed_parts, *first, *second, output)
        d_mixed_parts, barred = list(barred[:count]), barred[count:]
        first, second, output = halved(*barred[:2], 0), halved(*barred[2:4], 0), barred[4]

    d_packed_here, d_packed = [], []
    for block in range(blocks):
        (grads,) = attend_back(
            spot,
            qx_one,
            packed,
            mixed_here,
            [padded(part) for part in d_mixed_parts],
            None,
            heads,
            1,
            512,
            512,
            count,
            0,
            block,
        )
        grads = cut(grads)
        sent = [grads[:, far] for far in range(count)]
        if swift and block == 1:
            barred = together(grads, *d_packed_here, first[1], second[1], d_kv_two)
            grads, d_packed_here, d_kv_two = barred[0], [barred[1]], barred[4]
            first, second = (first[0], barred[2]), (second[0], barred[3])
            first, second = halved(*parted(first, 1), 2), halved(*parted(second, 1), 1)
            keep, send, gain_rows = grad_with_gain(
                where, normed_one[0], [d_packed_here[0][0], grads[0]], qkv_here, page_devices
            )
            grad_gain_one = jnp.sum(gain_rows, axis=1) / gain_one[0]
            gains = jnp.stack([grad_gain_one, grad_gain_two[0], grad_gain_three[0]])
            third, gains = halved_with(keep, send, gains, 0)
            barred = together(*sent, *d_packed)
            sent, d_packed = list(barred[:count]), list(barred[count:])
        elif swift:
            barred = together(*sent, grads, *d_mixed_parts, first[1], second[1])
            sent, grads = list(barred[:count]), barred[count]
            d_mixed_parts = list(barred[count + 1 : 2 * count + 1])
            first, second = (first[0], barred[-2]), (second[0], barred[-1])
            first, second = halved(*parted(first, 1), 1), halved(*parted(second, 2), 2)
        d_packed_here.append(grads)
        d_packed += ordered(received(sent), 3)
    d_key_two, d_value_two = (d_kv_two[:, 0, kind].reshape(-1, width) for kind in range(2))
    grad_patches = nt(d_key_two, kv_cross[:, :width]) + nt(d_value_two, kv_cross[:, width:])
    grad_patches = grad_patches.astype(jnp.bfloat16).reshape(pages, -1, width)
    if swift:
        grad_patches, both = together(grad_patches, both)
    grad_patches = lax.psum_scatter(grad_patches, "blk", scatter_dimension=1, tiled=True)

    if swift:
        rows_up = both.shape[0] // 2
        grad_w_up = (
            both[:rows_up]
            .reshape(-1, width // page_devices, both.shape[1])
            .transpose(1, 0, 2)
            .reshape(width // page_devices, -1)
        )
        grad_w_down = both[rows_up:]

        for bit in (1, 2):
            keep, send = parted(third, 1)
            if bit == 2:
                barred = together(send, *d_packed)
                send, d_packed = barred[0], list(barred[1:])
            third, gains = halved_with(keep, send, gains, bit)
        grad_tokens = leave(
            spot, d_packed, blocks, qkv_self, tokens, d_resid_one.reshape(tokens.shape), gain_one
        )
        qkv_part = added(*third)

        def piece(far):
            kv, rest = slice(far * 512, (far + 1) * 512), slice(far * 768, (far + 1) * 768)
            owner = (place + far) % count
            block = 3 * owner + (place - 3 * owner) % 4
            qkv = lax.dynamic_slice_in_dim(qkv_part, jnp.minimum(block // 4, 2) * 256, 256, 1)
            return [
                added(first[0][:, kv], first[1][:, kv]),
                added(second[0][:, rest], second[1][:, rest]),
                qkv,
            ]

        total = first[0][:, :512].astype(jnp.float32) + first[1][:, :512].astype(jnp.float32)
        rest = second[0][:, :768].astype(jnp.float32) + second[1][:, :768].astype(jnp.float32)
        total = jnp.concatenate([total, rest], 1)
        columns = jnp.zeros((qkv_part.shape[0], 4 * 256), jnp.bfloat16)
        columns = lax.dynamic_update_slice_in_dim(
            columns, piece(0)[2], (place - 3 * place) % 4 * 256, 1
        )
        pieces = together(
            gains, *(jnp.concatenate(piece(far), 1) for far in range(1, count))
        )
        gains, pieces = pieces[0], pieces[1:]
        all_gains = gains
        for far in far_first(count):
            got = shifted(pieces[far - 1], far)
            total += got[:, :1280].astype(jnp.float32)
            columns = lax.dynamic_update_slice_in_dim(
                columns, got[:, 1280:], (place - far - 3 * place) % 4 * 256, 1
            )
            all_gains += shifted(gains, far)
        gains = all_gains
        grad_kv_cross, grad_out_cross = total[:, :512], total[:, 512:768]
        grad_q_cross, grad_out_self = total[:, 768:1024], total[:, 1024:]
        grad_qkv_self = columns[:, :768].astype(jnp.float32)
    else:

        def over_rows(matrix):
            return lax.psum_scatter(
                matrix.astype(jnp.bfloat16), "page", scatter_dimension=0, tiled=True
            )

        def over_both(matrix):
            return lax.psum_scatter(
                over_rows(matrix), "blk", scatter_dimension=1, tiled=True
            ).astype(jnp.float32)

        grad_tokens = leave(
            spot, d_packed, blocks, qkv_self, tokens, d_resid_one.reshape(tokens.shape), gain_one
        )
        output = (resid_two + nn(active, w_down)).astype(jnp.bfloat16)
        output_patches = page_patches[:, :width]
        grad_w_up = over_both(tn(normed_three, d_upward))
        grad_w_down = over_both(tn(active, flat_cotangent))
        grad_out_cross = over_both(tn(flat_mixed_two, branch_two))
        grad_kv_cross = over_both(
            jnp.concatenate([tn(output_patches, d_key_two), tn(output_patches, d_value_two)], 1)
        )
        grad_q_cross = over_both(tn(normed_two, d_query_two))
        grad_out_self = over_both(tn(mixed_one, branch_one))
        d_packed_here = jnp.concatenate(d_packed_here, -1)
        columns = gathered([(d_packed_here[:, far], far) for far in range(count)], 2)
        columns = columns.transpose(0, 2, 1, 3).reshape(-1, 3 * own)
        grad_here = tn(normed_one.reshape(-1, width), columns)
        qkv_part = over_rows(grad_here)
        gain_rows = jnp.sum(grad_here * cut(qkv_here).astype(jnp.float32), axis=1)
        grad_gain_one = gain_rows / gain_one[0]
        gains = jnp.stack([grad_gain_one, grad_gain_two[0], grad_gain_three[0]])
        gains = lax.psum(gains, ("page", "blk"))
        qkv_rows = sent_to_all(qkv_part[None], 0)
        qkv_rows = qkv_rows.reshape(count, -1, 3, own).transpose(1, 2, 0, 3).reshape(-1, 3 * width)
        grad_qkv_self = lax.dynamic_slice_in_dim(
            qkv_rows, place * 3 * own, 3 * own, 1
        ).astype(jnp.float32)

    return (
        output.reshape(pages, token_count, width),
        grad_tokens,
        grad_patches.astype(jnp.float32),
        gains[0],
        grad_qkv_self,
        grad_out_self,
        gains[1],
        grad_q_cross,
        grad_kv_cross,
        grad_out_cross,
        gains[2],
        grad_w_up,
        grad_w_down,
    )


def solution(mesh):
    whole = P()
    cut = P("page", "blk", None)
    matrix = P("page", "blk")
    placed = (cut, cut, matrix) + (whole,) * 10 + (cut,)
    return jax.shard_map(
        on_device,
        mesh=mesh,
        in_specs=placed,
        out_specs=(
            cut,
            cut,
            cut,
            whole,
            matrix,
            matrix,
            whole,
            matrix,
            matrix,
            matrix,
            whole,
            matrix,
            matrix,
        ),
        check_vma=False,
    )
```
